32 devices in a mesh: rep: 16 (over z, y, x), tp: 2 (over core).
Axes of the slice: x: 2, y: 2, z: 4, core: 2. Of those that a mesh axis runs over, the one named last changes fastest.
Arguments:
- grads_narrow: bfloat16 [16, 1, 2, 1024, 512], P('rep', None, None, None, 'tp'), may hold values from -6 to 6
- errors_narrow: float32 [16, 1, 2, 1024, 512], P('rep', None, None, None, 'tp'), may hold values from -6 to 6
- starts_narrow: float32 [1, 2, 512, 32], P(None, None, 'tp'), may hold values from -6 to 6
- moment_narrow: float32 [1, 2, 524288], P(None, None, ('rep', 'tp')), may hold values from -0.75 to 0.75
- grads_square: bfloat16 [16, 1, 3, 1024, 1024], P('rep', None, None, None, 'tp'), may hold values from -6 to 6
- errors_square: float32 [16, 1, 3, 1024, 1024], P('rep', None, None, None, 'tp'), may hold values from -6 to 6
- starts_square: float32 [1, 3, 1024, 32], P(None, None, 'tp'), may hold values from -6 to 6
- moment_square: float32 [1, 3, 1048576], P(None, None, ('rep', 'tp')), may hold values from -0.75 to 0.75
Outputs:
- residue_narrow: float32 [16, 1, 2, 1024, 512], P('rep', None, None, None, 'tp')
- factor_narrow: float32 [1, 2, 512, 32], P(None, None, 'tp')
- velocity_narrow: float32 [1, 2, 524288], P(None, None, ('rep', 'tp'))
- residue_square: float32 [16, 1, 3, 1024, 1024], P('rep', None, None, None, 'tp')
- factor_square: float32 [1, 3, 1024, 32], P(None, None, 'tp')
- velocity_square: float32 [1, 3, 1048576], P(None, None, ('rep', 'tp'))
The draws below stay inside these ranges and needn't reach their ends.
All inputs are finite; a program needn't handle non-finite values.
Results may differ from the reference program's by a relative error of at most 0.0003.
Values sent between devices are 32-bit elements; how exact they have to be, the bound alone decides.
A program may use at most 128 MiB of HBM per device.

```python
import jax
import jax.numpy as jnp
from jax import lax

D = 1024
DK = 512
R = 32
ROUNDS = 2
NS_STEPS = 5
LAYERS = 1
REPLICAS = 16
N_REP = 16


def raised(drawn, own_key, source, target, parts, factor):
    def block_of(dim):
        return (jnp.arange(drawn.shape[dim]) // (drawn.shape[dim] // parts)).reshape((-1,) + (1,) * (drawn.ndim - 1 - dim))

    one_side = jax.random.permutation(own_key, parts)[block_of(target)]
    other_side = (block_of(target) + parts // 2) % parts
    return jnp.where((block_of(source) == one_side) | (block_of(source) == other_side), factor * drawn, drawn)


def shard_levels(stream_key, extent, shards, low, top_value):
    gain, own = 1.0, jax.random.fold_in(stream_key, 6)
    for position, shards_of in shards:
        draws = jnp.exp(jax.random.uniform(jax.random.fold_in(own, position), (shards_of,), jnp.float32, low / len(shards), top_value / len(shards)))
        gain = gain * jnp.repeat(draws, extent[position] // shards_of).reshape([-1 if axis == position else 1 for axis in range(len(extent))])
    return gain


def normal_values(rng, shape, spread, reach, pieces=(), dtype=jnp.bfloat16):
    gain = shard_levels(rng, shape, pieces, -0.22, 0.18) if pieces else 1.0
    drawn = jax.random.normal(rng, shape, jnp.float32) * spread * gain
    return jnp.minimum(jnp.maximum(drawn, -reach), reach).astype(dtype)


def heavy_noise(rng, dims, scale, bound, pieces, heavy, kind=jnp.bfloat16):
    drawn = scale * jax.random.normal(rng, dims, jnp.float32)
    if pieces:
        drawn = drawn * shard_levels(rng, dims, pieces, -0.22, 0.18)
    return jnp.clip(raised(drawn, jax.random.fold_in(rng, 3), *heavy), -bound, bound).astype(kind)


def setup_inputs(seed: int = 0) -> dict:
    key_list = jax.random.split(jax.random.key(seed), 9)
    grads_narrow = heavy_noise(key_list[0], (REPLICAS, LAYERS, 2, D, DK), 1.0, 6.0, ((0, 16), (4, 2)), (0, 3, 16, 2.0))
    errors_narrow = normal_values(key_list[1], (REPLICAS, LAYERS, 2, D, DK), 0.5, 6.0, ((0, 16), (4, 2)), jnp.float32)
    starts_narrow = normal_values(key_list[2], (LAYERS, 2, DK, R), 1.0, 6.0, ((2, 2),), jnp.float32)
    moment_narrow = normal_values(key_list[3], (LAYERS, 2, D * DK), 0.05, 0.75, ((2, 32),), jnp.float32)
    grads_square = heavy_noise(key_list[4], (REPLICAS, LAYERS, 3, D, D), 1.0, 6.0, ((0, 16), (4, 2)), (0, 3, 16, 2.0))
    errors_square = normal_values(key_list[5], (REPLICAS, LAYERS, 3, D, D), 0.5, 6.0, ((0, 16), (4, 2)), jnp.float32)
    starts_square = normal_values(key_list[6], (LAYERS, 3, D, R), 1.0, 6.0, ((2, 2),), jnp.float32)
    moment_square = normal_values(key_list[7], (LAYERS, 3, D * D), 0.05, 0.75, ((2, 32),), jnp.float32)
    return dict(grads_narrow=grads_narrow, errors_narrow=errors_narrow, starts_narrow=starts_narrow, moment_narrow=moment_narrow, grads_square=grads_square, errors_square=errors_square, starts_square=starts_square, moment_square=moment_square)


epsilon = 1e-06
momentum_decay = 0.9
highest = lax.Precision.HIGHEST

def orthonormal(panel):
    scaled = panel / (jnp.sqrt(jnp.sum(panel * panel)) + epsilon)
    for sweep in range(NS_STEPS):
        gram = lax.dot_general(scaled, scaled, (((0,), (0,)), ((), ())), precision=highest)
        scaled = 1.5 * scaled - 0.5 * jnp.dot(scaled, gram, precision=highest)
    return scaled

def compress(grads, errors, start, moment):
    merged = grads.astype(jnp.float32) + errors
    factor = start
    ortho = None
    for turn in range(ROUNDS):
        panel = jnp.einsum('rdn,nk->dk', merged, factor, precision=highest)
        ortho = orthonormal(panel)
        factor = jnp.einsum('rdn,dk->nk', merged, ortho, precision=highest) / N_REP
    approx = lax.dot_general(ortho, factor, (((1,), (1,)), ((), ())), precision=highest)
    residue = merged - approx[None]
    velocity = momentum_decay * moment + approx.reshape(-1)
    return (residue, factor, velocity)

def group(grads, errors, starts, moment, count):
    residues, factors, velocities = ([], [], [])
    for layer in range(LAYERS):
        res_layer, fac_layer, vel_layer = ([], [], [])
        for which in range(count):
            res, fac, vel = compress(grads[:, layer, which], errors[:, layer, which], starts[layer, which], moment[layer, which])
            res_layer.append(res)
            fac_layer.append(fac)
            vel_layer.append(vel)
        residues.append(jnp.stack(res_layer, axis=1))
        factors.append(jnp.stack(fac_layer, axis=0))
        velocities.append(jnp.stack(vel_layer, axis=0))
    return (jnp.stack(residues, axis=1), jnp.stack(factors, axis=0), jnp.stack(velocities, axis=0))

def reference(grads_narrow, errors_narrow, starts_narrow, moment_narrow, grads_square, errors_square, starts_square, moment_square):
    res_n, fac_n, vel_n = group(grads_narrow, errors_narrow, starts_narrow, moment_narrow, 2)
    res_s, fac_s, vel_s = group(grads_square, errors_square, starts_square, moment_square, 3)
    return (res_n, fac_n, vel_n, res_s, fac_s, vel_s)
```

```python
import functools

import jax
import jax.numpy as jnp
from jax import lax
from jax.experimental import pallas as pl
from jax.experimental.pallas import tpu as pltpu
from jax.sharding import PartitionSpec as P

ROUNDS = 2
NS_STEPS = 5
LANES = 128
BAND = 256
VMEM_LIMIT = 44 * 1024 * 1024
LAST_LIMIT = 24 * 1024 * 1024

epsilon = 1e-06
momentum_decay = 0.9
highest = lax.Precision.HIGHEST
f32, bf16 = jnp.float32, jnp.bfloat16
MESH = pl.DeviceIdType.MESH


def split(x):
    hi = x.astype(bf16)
    lo = (x - hi.astype(f32)).astype(bf16)
    return hi, lo


def dot(a, b, dims, precision=None):
    return lax.dot_general(a, b, (dims, ((), ())), precision=precision, preferred_element_type=f32)


NN, NT, TN = ((1,), (0,)), ((1,), (1,)), ((0,), (0,))


def rows_at(at, size, unit=8):
    return pl.ds(pl.multiple_of(at, unit), size)


def first_blocks(widths):
    first, at = [], 0
    for width in widths:
        first.append(at)
        at += width // LANES
    return first, at


def factor_of(ref, first, width, rank, offset=0):
    pieces = [
        ref[(offset + first + b) * rank : (offset + first + b + 1) * rank, :]
        for b in range(width // LANES)
    ]
    return jnp.concatenate(pieces, axis=1)


def items_of(square, narrow):
    return [(0, which) for which in range(square)] + [(1, which) for which in range(narrow)]


def groups_of(widths):
    half, total, cut = sum(widths) / 2, 0, len(widths)
    for at, width in enumerate(widths):
        if total >= half:
            cut = at
            break
        total += width
    return [range(0, cut), range(cut, len(widths))] if cut < len(widths) else [range(len(widths))]


def share_of(rows, replicas):
    return -(-rows // (8 * replicas)) * 8


class Group:
    names = (
        "send", "inbox", "mine", "panel", "land", "part", "total", "landq", "turn",
        "side", "rs_send", "rs_recv", "ag_send", "ag_recv",
    )

    def __init__(self, items, refs):
        self.items = items
        for name, ref in zip(self.names, refs):
            setattr(self, name, ref)


def main_kernel(rank, replicas, runs, *refs):
    gs, es, ss, gn, en, sn, hs, ls, hn, ln, ortho, both = refs[:12]
    stage_gs, stage_es, stage_gn, stage_en, fs, fn, load_sem = refs[12:19]
    per = len(Group.names)
    groups = [Group(run, refs[19 + per * k : 19 + per * (k + 1)]) for k, run in enumerate(runs)]
    rep, tp = lax.axis_index("rep"), lax.axis_index("tp")
    other = {"rep": rep, "tp": 1 - tp}
    part = hs.shape[1] // 2
    blocks = part // LANES
    kinds = ((gs, es, ss, hs, ls, stage_gs, stage_es, fs), (gn, en, sn, hn, ln, stage_gn, stage_en, fn))
    items = items_of(hs.shape[0], hn.shape[0])
    widths = [kinds[kind][3].shape[2] for kind, _ in items]
    first_block, all_blocks = first_blocks(widths)

    def peer(j):
        return {"rep": lax.rem(rep + j, replicas), "tp": tp}

    loads, count = {}, 0
    for group in groups:
        for where, half in enumerate((1 - tp, tp)):
            rows = rows_at(half * part, part, LANES)
            for item in group.items:
                kind, which = items[item]
                g, e, _, _, _, sg, se, _ = kinds[kind]
                loads[item, where] = []
                for src, dst in ((g, sg), (e, se)):
                    copy = pltpu.make_async_copy(src.at[which, rows], dst.at[which, rows], load_sem.at[count])
                    copy.start()
                    loads[item, where].append(copy)
                    count += 1

    barrier = pltpu.get_barrier_semaphore()

    def greet(j, carry):
        pl.semaphore_signal(barrier, inc=1, device_id=peer(j), device_id_type=MESH)
        return carry

    lax.fori_loop(1, replicas, greet, 0)
    pl.semaphore_signal(barrier, inc=1, device_id=other, device_id_type=MESH)

    for kind, which in items:
        start, keep = kinds[kind][2], kinds[kind][7]
        keep[which] = jnp.concatenate(split(start[which]), axis=0)

    def to_all(source, target, sends, recvs):
        def copy_of(j):
            return pltpu.make_async_remote_copy(
                src_ref=source(j), dst_ref=target(j), send_sem=sends.at[j], recv_sem=recvs.at[j],
                device_id=peer(j), device_id_type=MESH,
            )

        def begin(j, carry):
            copy_of(j).start()
            return carry

        def end(j, carry):
            copy_of(j).wait()
            return carry

        lax.fori_loop(replicas // 2, replicas, begin, 0)
        lax.fori_loop(1, replicas // 2, begin, 0)
        return lambda: lax.fori_loop(1, replicas, end, 0)

    def scatter(group, mine, land):
        share = land.shape[1]
        return to_all(
            lambda j: mine.at[rows_at(lax.rem(rep + j, replicas) * share, share)],
            lambda j: land.at[j - 1], group.rs_send, group.rs_recv,
        )

    def gather(group, whole, share):
        view = whole.at[rows_at(rep * share, share)]
        return to_all(lambda j: view, lambda j: view, group.ag_send, group.ag_recv)

    def add_up(mine, land, whole):
        share = land.shape[1]
        own = rows_at(rep * share, share)
        value = mine[own, :]
        for j in range(replicas - 1):
            value = value + land[j]
        whole[own, :] = value

    def to_sibling(group, at, src, dst):
        copy = pltpu.make_async_remote_copy(
            src_ref=src, dst_ref=dst, send_sem=group.side.at[2 * at], recv_sem=group.side.at[2 * at + 1],
            device_id=other, device_id_type=MESH,
        )
        copy.start()
        return copy

    def left_half(group, half, out, where, fresh):
        size = len(group.items) * rank
        for place, item in enumerate(group.items):
            kind, which = items[item]
            _, _, _, h, l, sg, se, keep = kinds[kind]
            if fresh:
                for copy in loads[item, where]:
                    copy.wait()
            stacked = keep[which]
            for band in range(part // BAND):
                rows = rows_at(half * part + band * BAND, BAND, LANES)
                if fresh:
                    hi, lo = split(sg[which, rows, :].astype(f32) + se[which, rows, :])
                    h[which, rows, :], l[which, rows, :] = hi, lo
                else:
                    hi, lo = h[which, rows, :], l[which, rows, :]
                twice = dot(stacked, hi, NT)
                result = twice[:rank] + twice[rank:] + dot(stacked[:rank], lo, NT)
                for b in range(BAND // LANES):
                    at = (band * (BAND // LANES) + b) * size + place * rank
                    out[at : at + rank, :] = result[:, b * LANES : (b + 1) * LANES]

    def panel_half(group, half):
        size = len(group.items) * rank
        return [group.panel[half, b * size : (b + 1) * size, :] for b in range(blocks)]

    def right_half(group, half, first):
        wide = jnp.concatenate(panel_half(group, half), axis=1)
        rows = rows_at(half * part, part, LANES)
        at = 0
        for place, item in enumerate(group.items):
            kind, which = items[item]
            h, l = kinds[kind][3:5]
            hi, lo = split(wide[place * rank : (place + 1) * rank])
            twice = dot(jnp.concatenate([hi, lo], axis=0), h[which, rows, :], NN)
            term = twice[:rank] + twice[rank:] + dot(hi, l[which, rows, :], NN)
            for b in range(widths[item] // LANES):
                piece = term[:, b * LANES : (b + 1) * LANES]
                if first:
                    group.part[at : at + rank, :] = piece
                else:
                    group.part[at : at + rank, :] += piece
                at += rank

    def orthonormal(group, final):
        size = len(group.items) * rank
        stacked = jnp.concatenate(panel_half(group, 0) + panel_half(group, 1), axis=1)
        row = lax.broadcasted_iota(jnp.int32, (size, size), 0)
        column = lax.broadcasted_iota(jnp.int32, (size, size), 1)
        own = (row // rank) == (column // rank)
        identity = jnp.where(row == column, 1.0, 0.0).astype(f32)
        scale, scaled = [], []
        for place in range(len(group.items)):
            piece = stacked[place * rank : (place + 1) * rank]
            by = 1.0 / (jnp.sqrt(jnp.sum(piece * piece)) + epsilon)
            scale.append(jnp.full((rank, size), by, f32))
            scaled.append(piece * by)
        scaled = jnp.concatenate(scaled, axis=0)
        gram = jnp.where(own, dot(scaled, scaled, NT, highest), 0.0)
        total = None
        for sweep in range(NS_STEPS):
            turn = 1.5 * identity - 0.5 * gram
            total = turn if total is None else dot(turn, total, NN, highest)
            if sweep < NS_STEPS - 1:
                gram = dot(dot(turn, gram, NN, highest), turn, NN, highest)
        group.turn[...] = total * jnp.concatenate(scale, axis=0)
        if final:
            result = dot(total, scaled, NN, highest)
            base = group.items[0] * rank
            for b in range(2 * blocks):
                ortho[b, base : base + size, :] = result[:, b * LANES : (b + 1) * LANES]

    def factors(group):
        at, result = 0, []
        for place, item in enumerate(group.items):
            own = slice(place * rank, (place + 1) * rank)
            pieces = []
            for b in range(widths[item] // LANES):
                pieces.append(group.total[at : at + rank, :])
                at += rank
            turned = dot(group.turn[own, own] / replicas, jnp.concatenate(pieces, axis=1), NN, highest)
            result.append(turned)
        return result

    pl.semaphore_wait(barrier, replicas)
    finish = [None] * len(groups)
    for turn in range(ROUNDS):
        final = turn == ROUNDS - 1
        for k, group in enumerate(groups):
            if turn:
                finish[k]()
                for item, whole in zip(group.items, factors(group)):
                    kind, which = items[item]
                    kinds[kind][7][which] = jnp.concatenate(split(whole), axis=0)
            left_half(group, 1 - tp, group.send, 0, not turn)
            across = to_sibling(group, 0, group.send, group.inbox)
            left_half(group, tp, group.mine, 1, not turn)
            across.wait()
            used = group.inbox.shape[0]
            group.mine[0:used, :] += group.inbox[...]
            finish[k] = scatter(group, group.mine, group.land)
        for k, group in enumerate(groups):
            finish[k]()
            whole = group.panel.at[tp]
            add_up(group.mine, group.land, whole)
            finish[k] = gather(group, whole, group.land.shape[1])
        for k, group in enumerate(groups):
            finish[k]()
            across = to_sibling(group, 1, group.panel.at[tp], group.panel.at[tp])
            right_half(group, tp, True)
            across.wait()
            right_half(group, 1 - tp, False)
            finish[k] = scatter(group, group.part, group.landq)
        for k, group in enumerate(groups):
            orthonormal(group, final)
            finish[k]()
            add_up(group.part, group.landq, group.total)
            finish[k] = gather(group, group.total, group.landq.shape[1])
    for k, group in enumerate(groups):
        finish[k]()
        base = (tp * all_blocks + first_block[group.items[0]]) * rank
        at = 0
        for item, whole in zip(group.items, factors(group)):
            for b in range(widths[item] // LANES):
                both[rows_at(base + at, rank), :] = whole[:, b * LANES : (b + 1) * LANES]
                at += rank
        view = both.at[rows_at(base, at)]
        finish[k] = to_sibling(group, 2, view, view)
    for across in finish:
        across.wait()


def last_kernel(rank, ortho, both, hs, ls, hn, ln, ms, mn, rs, rn, fs, fn, vs, vn, ks, kn, rows_s, rows_n):
    step = pl.program_id(0)
    counts = (hs.shape[0], hn.shape[0])
    widths = [hs.shape[2]] * counts[0] + [hn.shape[2]] * counts[1]
    first, blocks = first_blocks(widths)
    tp = lax.axis_index("tp")
    place = lax.axis_index("rep") * lax.axis_size("tp") + tp
    own = pl.multiple_of(tp * blocks * rank, blocks * rank)

    def wide(whole):
        hi, lo = split(whole)
        return jnp.concatenate([hi, hi, lo], axis=0)

    def tall(part):
        hi, lo = split(part)
        return jnp.concatenate([hi, lo, hi], axis=0)

    @pl.when(step == 0)
    def _():
        item = 0
        for f, k, m, v, rows_ref in ((fs, ks, ms, vs, rows_s), (fn, kn, mn, vn, rows_n)):
            per_row = rows_ref.shape[0]
            rows = m.shape[0] // (f.shape[0] * per_row)
            interleaved = f is fn
            at = place * rows
            block, inside = at // LANES, lax.rem(at, LANES)
            for which in range(f.shape[0]):
                width = widths[item]
                pieces = [
                    both[pl.ds(own + (first[item] + b) * rank, rank), :]
                    for b in range(width // LANES)
                ]
                mine = jnp.concatenate(pieces, axis=1)
                f[which] = mine
                k[which] = wide(mine)
                full = jnp.concatenate(
                    [factor_of(both, first[item], width, rank, core * blocks) for core in range(2)],
                    axis=1,
                )
                left = tall(ortho[block, item * rank : (item + 1) * rank, :])
                approx = dot(left, wide(full), TN)
                for c in range(per_row):
                    rows_ref[c] = approx[:, c * LANES : (c + 1) * LANES]
                for c in range(per_row):
                    if interleaved:
                        spot = pl.ds(c * f.shape[0] + which, rows, stride=per_row * f.shape[0])
                    else:
                        spot = pl.ds(which * rows * per_row + c, rows, stride=per_row)
                    v[spot, :] = (
                        momentum_decay * m[spot, :]
                        + rows_ref[c, pl.ds(pl.multiple_of(inside, 8), rows), :]
                    )
                item += 1

    per = BAND // LANES
    band = jnp.concatenate([ortho[step * per + b] for b in range(per)], axis=1)
    item = 0
    for h, l, k, r in ((hs, ls, ks, rs), (hn, ln, kn, rn)):
        for which in range(h.shape[0]):
            left = tall(band[item * rank : (item + 1) * rank])
            approx = dot(left, k[which], TN)
            r[which] = (h[which].astype(f32) + l[which].astype(f32)) - approx
            item += 1


def on_device(gn, en, sn, mn, gs, es, ss, ms):
    replicas = lax.axis_size("rep")
    shape_gn, shape_gs, shape_sn, shape_ss = gn.shape, gs.shape, sn.shape, ss.shape
    shape_mn, shape_ms = mn.shape, ms.shape
    gn, en, gs, es = (
        x.reshape((x.shape[1] * x.shape[2],) + x.shape[3:]) for x in (gn, en, gs, es)
    )
    sn, ss = (jnp.swapaxes(x.reshape((-1,) + x.shape[2:]), 1, 2) for x in (sn, ss))
    cn, depth, wn = gn.shape
    cs, _, ws = gs.shape
    rank = sn.shape[1]
    items = cn + cs
    steps, per, blocks = depth // BAND, BAND // LANES, depth // LANES
    widths = [ws] * cs + [wn] * cn
    _, all_blocks = first_blocks(widths)
    mn = jnp.swapaxes(mn.reshape(cn, -1, LANES), 0, 1).reshape(-1, LANES)
    ms = ms.reshape(-1, LANES)
    runs = groups_of(widths)

    in_vmem = pl.BlockSpec(memory_space=pltpu.VMEM)
    in_hbm = pl.BlockSpec(memory_space=pltpu.HBM)

    def group_scratch(run):
        size = len(run) * rank
        half_rows, q_rows = blocks // 2 * size, sum(widths[i] for i in run) // LANES * rank
        share, share_q = share_of(half_rows, replicas), share_of(q_rows, replicas)
        return [
            pltpu.VMEM((half_rows, LANES), f32),
            pltpu.VMEM((half_rows, LANES), f32),
            pltpu.VMEM((share * replicas, LANES), f32),
            pltpu.VMEM((2, share * replicas, LANES), f32),
            pltpu.VMEM((replicas - 1, share, LANES), f32),
            pltpu.VMEM((share_q * replicas, LANES), f32),
            pltpu.VMEM((share_q * replicas, LANES), f32),
            pltpu.VMEM((replicas - 1, share_q, LANES), f32),
            pltpu.VMEM((size, size), f32),
            pltpu.SemaphoreType.DMA((6,)),
        ] + [pltpu.SemaphoreType.DMA((replicas,)) for _ in range(4)]

    scratch = [
        pltpu.VMEM(gs.shape, bf16),
        pltpu.VMEM(gs.shape, f32),
        pltpu.VMEM(gn.shape, bf16),
        pltpu.VMEM(gn.shape, f32),
        pltpu.VMEM((cs, 2 * rank, ws), bf16),
        pltpu.VMEM((cn, 2 * rank, wn), bf16),
        pltpu.SemaphoreType.DMA((4 * items,)),
    ]
    for run in runs:
        scratch += group_scratch(run)
    panel_shape = jax.ShapeDtypeStruct((blocks, items * rank, LANES), f32)
    factor_shape = jax.ShapeDtypeStruct((2 * all_blocks * rank, LANES), f32)
    hs, ls, hn, ln, ortho, both = pl.pallas_call(
        functools.partial(main_kernel, rank, replicas, runs),
        in_specs=[in_hbm, in_hbm, in_vmem, in_hbm, in_hbm, in_vmem],
        out_specs=[in_vmem] * 6,
        out_shape=[jax.ShapeDtypeStruct(x.shape, bf16) for x in (gs, gs, gn, gn)]
        + [panel_shape, factor_shape],
        scratch_shapes=scratch,
        compiler_params=pltpu.CompilerParams(
            collective_id=0, has_side_effects=True, vmem_limit_bytes=VMEM_LIMIT
        ),
        name="rounds",
    )(gs, es, ss, gn, en, sn)

    band_n = pl.BlockSpec((cn, BAND, wn), lambda t: (0, t, 0))
    band_s = pl.BlockSpec((cs, BAND, ws), lambda t: (0, t, 0))

    def full(shape):
        return pl.BlockSpec(shape, lambda t: (0,) * len(shape))

    rs, rn, fs, fn, vs, vn = pl.pallas_call(
        functools.partial(last_kernel, rank),
        grid=(steps,),
        in_specs=[full(panel_shape.shape), full(factor_shape.shape)]
        + [band_s, band_s, band_n, band_n]
        + [full(ms.shape), full(mn.shape)],
        out_specs=[
            band_s, band_n, full(ss.shape), full(sn.shape), full(ms.shape), full(mn.shape),
        ],
        out_shape=[
            jax.ShapeDtypeStruct(x.shape, f32) for x in (gs, gn, ss, sn, ms, mn)
        ],
        scratch_shapes=[
            pltpu.VMEM((cs, 3 * rank, ws), bf16),
            pltpu.VMEM((cn, 3 * rank, wn), bf16),
            pltpu.VMEM((2 * ws // LANES, LANES, LANES), f32),
            pltpu.VMEM((2 * wn // LANES, LANES, LANES), f32),
        ],
        compiler_params=pltpu.CompilerParams(vmem_limit_bytes=LAST_LIMIT),
        name="last",
    )(ortho, both, hs, ls, hn, ln, ms, mn)
    return (
        rn.reshape(shape_gn),
        jnp.swapaxes(fn, 1, 2).reshape(shape_sn),
        jnp.swapaxes(vn.reshape(-1, cn, LANES), 0, 1).reshape(shape_mn),
        rs.reshape(shape_gs),
        jnp.swapaxes(fs, 1, 2).reshape(shape_ss),
        vs.reshape(shape_ms),
    )


def solution(mesh):
    in_specs = (
        P("rep", None, None, None, "tp"),
        P("rep", None, None, None, "tp"),
        P(None, None, "tp", None),
        P(None, None, ("rep", "tp")),
        P("rep", None, None, None, "tp"),
        P("rep", None, None, None, "tp"),
        P(None, None, "tp", None),
        P(None, None, ("rep", "tp")),
    )
    out_specs = (
        P("rep", None, None, None, "tp"),
        P(None, None, "tp", None),
        P(None, None, ("rep", "tp")),
        P("rep", None, None, None, "tp"),
        P(None, None, "tp", None),
        P(None, None, ("rep", "tp")),
    )
    return jax.shard_map(
        on_device, mesh=mesh, in_specs=in_specs, out_specs=out_specs, check_vma=False
    )
```

```python
import functools

import jax
import jax.numpy as jnp
from jax import lax
from jax.experimental import pallas as pl
from jax.experimental.pallas import tpu as pltpu
from jax.sharding import PartitionSpec as P

ROUNDS = 2
NS_STEPS = 5
LANES = 128
BAND = 256
NEAR = 8
VMEM_LIMIT = 40 * 1024 * 1024
LAST_LIMIT = 24 * 1024 * 1024

epsilon = 1e-06
momentum_decay = 0.9
highest = lax.Precision.HIGHEST
f32, bf16 = jnp.float32, jnp.bfloat16
MESH = pl.DeviceIdType.MESH


def split(x):
    hi = x.astype(bf16)
    lo = (x - hi.astype(f32)).astype(bf16)
    return hi, lo


def dot(a, b, dims, precision=None):
    return lax.dot_general(a, b, (dims, ((), ())), precision=precision, preferred_element_type=f32)


NN, NT, TN = ((1,), (0,)), ((1,), (1,)), ((0,), (0,))


def rows_at(at, size, unit=8):
    return pl.ds(pl.multiple_of(at, unit), size)


def first_blocks(widths):
    first, at = [], 0
    for width in widths:
        first.append(at)
        at += width // LANES
    return first, at


def factor_of(ref, first, width, rank, offset=0):
    pieces = [
        ref[(offset + first + b) * rank : (offset + first + b + 1) * rank, :]
        for b in range(width // LANES)
    ]
    return jnp.concatenate(pieces, axis=1)


def items_of(square, narrow):
    return [(0, which) for which in range(square)] + [(1, which) for which in range(narrow)]


def groups_of(widths):
    half, total, cut = sum(widths) / 2, 0, len(widths)
    for at, width in enumerate(widths):
        if total >= half:
            cut = at
            break
        total += width
    return [range(0, cut), range(cut, len(widths))] if cut < len(widths) else [range(len(widths))]


def share_of(rows, parts):
    return -(-rows // (8 * parts)) * 8


def near_size(replicas):
    return NEAR if replicas % NEAR == 0 else replicas


class Group:
    names = (
        "send", "inbox", "mine", "panel", "land", "cross", "part", "total", "landq", "crossq", "turn",
        "side", "rs_send", "rs_recv", "ag_send", "ag_recv", "x_send", "x_recv", "xq_send", "xq_recv",
    )

    def __init__(self, items, refs):
        self.items = items
        for name, ref in zip(self.names, refs):
            setattr(self, name, ref)


def main_kernel(rank, replicas, runs, *refs):
    gs, es, ss, gn, en, sn, out_s, out_n, ortho, both = refs[:10]
    stage_gs, stage_es, stage_ss, hs, ls, fs, stage_gn, stage_en, stage_sn, hn, ln, fn = refs[10:22]
    load_sem, start_sem, save_sem = refs[22:25]
    per = len(Group.names)
    groups = [Group(run, refs[25 + per * k : 25 + per * (k + 1)]) for k, run in enumerate(runs)]
    rep, tp = lax.axis_index("rep"), lax.axis_index("tp")
    other = {"rep": rep, "tp": 1 - tp}
    part = hs.shape[1] // 2
    blocks = part // LANES
    kinds = (
        (gs, es, stage_ss, hs, ls, stage_gs, stage_es, fs),
        (gn, en, stage_sn, hn, ln, stage_gn, stage_en, fn),
    )
    items = items_of(hs.shape[0], hn.shape[0])
    widths = [kinds[kind][3].shape[2] for kind, _ in items]
    first_block, all_blocks = first_blocks(widths)

    near = near_size(replicas)
    far = replicas // near
    near_at, far_at = lax.rem(rep, near), rep // near
    near_order = sorted(range(1, near), key=lambda j: -bin(j).count("1"))

    def near_of(j):
        result, bit = 0, 1
        while bit < near:
            here = lax.rem(near_at // bit, 2)
            result = result + bit * (1 - here if j & bit else here)
            bit *= 2
        return result

    def near_peer(j):
        return {"rep": far_at * near + near_of(j), "tp": tp}

    def far_peer(j):
        return {"rep": lax.rem(far_at + j, far) * near + near_at, "tp": tp}

    barrier = pltpu.get_barrier_semaphore()

    partners = [near_peer(j) for j in near_order] + [far_peer(j) for j in range(1, far)] + [other]
    for partner in partners:
        pl.semaphore_signal(barrier, inc=1, device_id=partner, device_id_type=MESH)

    starts = [
        pltpu.make_async_copy(src, dst, start_sem.at[i])
        for i, (src, dst) in enumerate(((ss, stage_ss), (sn, stage_sn)))
    ]
    for copy in starts:
        copy.start()
    loads, count, saves = {}, 0, []
    for group in groups:
        for where, half in enumerate((1 - tp, tp)):
            rows = rows_at(half * part, part, LANES)
            for item in group.items:
                kind, which = items[item]
                g, e, _, _, _, sg, se, _ = kinds[kind]
                loads[item, where] = []
                for src, dst in ((g, sg), (e, se)):
                    copy = pltpu.make_async_copy(src.at[which, rows], dst.at[which, rows], load_sem.at[count])
                    copy.start()
                    loads[item, where].append(copy)
                    count += 1

    for copy in starts:
        copy.wait()
    for kind, which in items:
        start, keep = kinds[kind][2], kinds[kind][7]
        keep[which] = jnp.concatenate(split(start[which]), axis=0)

    def spread(order, source, target, sends, recvs, to):
        copies = []
        for j in order:
            copy = pltpu.make_async_remote_copy(
                src_ref=source(j), dst_ref=target(j), send_sem=sends.at[j], recv_sem=recvs.at[j],
                device_id=to(j), device_id_type=MESH,
            )
            copy.start()
            copies.append(copy)
        return copies

    def wait_all(copies):
        for copy in copies:
            copy.wait()

    def scatter(group, mine, land):
        share = land.shape[1]
        return spread(
            near_order, lambda j: mine.at[rows_at(near_of(j) * share, share)], lambda j: land.at[j - 1],
            group.rs_send, group.rs_recv, near_peer,
        )

    def trade(mine, land, cross, sends, recvs):
        share = land.shape[1]
        own = rows_at(near_at * share, share)
        value = mine[own, :]
        for j in range(near - 1):
            value = value + land[j]
        cross[far_at] = value
        view = cross.at[far_at]
        return spread(range(1, far), lambda j: view, lambda j: view, sends, recvs, far_peer)

    def gather(group, cross, whole):
        share = cross.shape[1]
        own = rows_at(near_at * share, share)
        value = cross[0]
        for j in range(1, far):
            value = value + cross[j]
        whole[own, :] = value
        view = whole.at[own]
        return spread(near_order, lambda j: view, lambda j: view, group.ag_send, group.ag_recv, near_peer)

    def to_sibling(group, at, src, dst):
        copy = pltpu.make_async_remote_copy(
            src_ref=src, dst_ref=dst, send_sem=group.side.at[2 * at], recv_sem=group.side.at[2 * at + 1],
            device_id=other, device_id_type=MESH,
        )
        copy.start()
        return copy

    def left_half(group, half, out, where, fresh):
        size = len(group.items) * rank
        for place, item in enumerate(group.items):
            kind, which = items[item]
            _, _, _, h, l, sg, se, keep = kinds[kind]
            if fresh:
                for copy in loads[item, where]:
                    copy.wait()
            stacked = keep[which]
            for band in range(part // BAND):
                rows = rows_at(half * part + band * BAND, BAND, LANES)
                if fresh:
                    merged = sg[which, rows, :].astype(f32) + se[which, rows, :]
                    hi, lo = split(merged)
                    se[which, rows, :], h[which, rows, :], l[which, rows, :] = merged, hi, lo
                else:
                    hi, lo = h[which, rows, :], l[which, rows, :]
                twice = dot(stacked, hi, NT)
                result = twice[:rank] + twice[rank:] + dot(stacked[:rank], lo, NT)
                for b in range(BAND // LANES):
                    at = (band * (BAND // LANES) + b) * size + place * rank
                    out[at : at + rank, :] = result[:, b * LANES : (b + 1) * LANES]
            if fresh:
                rows = rows_at(half * part, part, LANES)
                target = (out_s, out_n)[kind]
                copy = pltpu.make_async_copy(se.at[which, rows], target.at[which, rows], save_sem.at[len(saves)])
                copy.start()
                saves.append(copy)

    def panel_half(group, half):
        size = len(group.items) * rank
        return [group.panel[half, b * size : (b + 1) * size, :] for b in range(blocks)]

    def right_half(group, half, first):
        wide = jnp.concatenate(panel_half(group, half), axis=1)
        rows = rows_at(half * part, part, LANES)
        at = 0
        for place, item in enumerate(group.items):
            kind, which = items[item]
            h, l = kinds[kind][3:5]
            hi, lo = split(wide[place * rank : (place + 1) * rank])
            twice = dot(jnp.concatenate([hi, lo], axis=0), h[which, rows, :], NN)
            term = twice[:rank] + twice[rank:] + dot(hi, l[which, rows, :], NN)
            for b in range(widths[item] // LANES):
                piece = term[:, b * LANES : (b + 1) * LANES]
                if first:
                    group.part[at : at + rank, :] = piece
                else:
                    group.part[at : at + rank, :] += piece
                at += rank

    def orthonormal(group, final):
        size = len(group.items) * rank
        stacked = jnp.concatenate(panel_half(group, 0) + panel_half(group, 1), axis=1)
        row = lax.broadcasted_iota(jnp.int32, (size, size), 0)
        column = lax.broadcasted_iota(jnp.int32, (size, size), 1)
        own = (row // rank) == (column // rank)
        identity = jnp.where(row == column, 1.0, 0.0).astype(f32)
        scale, scaled = [], []
        for place in range(len(group.items)):
            piece = stacked[place * rank : (place + 1) * rank]
            by = 1.0 / (jnp.sqrt(jnp.sum(piece * piece)) + epsilon)
            scale.append(jnp.full((rank, size), by, f32))
            scaled.append(piece * by)
        scaled = jnp.concatenate(scaled, axis=0)
        gram = jnp.where(own, dot(scaled, scaled, NT, highest), 0.0)
        total = None
        for sweep in range(NS_STEPS):
            turn = 1.5 * identity - 0.5 * gram
            total = turn if total is None else dot(turn, total, NN, highest)
            if sweep < NS_STEPS - 1:
                gram = dot(dot(turn, gram, NN, highest), turn, NN, highest)
        group.turn[...] = total * jnp.concatenate(scale, axis=0)
        if final:
            result = dot(total, scaled, NN, highest)
            base = group.items[0] * rank
            for b in range(2 * blocks):
                ortho[b, base : base + size, :] = result[:, b * LANES : (b + 1) * LANES]

    def factors(group):
        at, result = 0, []
        for place, item in enumerate(group.items):
            own = slice(place * rank, (place + 1) * rank)
            pieces = []
            for b in range(widths[item] // LANES):
                pieces.append(group.total[at : at + rank, :])
                at += rank
            turned = dot(group.turn[own, own] / replicas, jnp.concatenate(pieces, axis=1), NN, highest)
            result.append(turned)
        return result

    pl.semaphore_wait(barrier, len(partners))
    flight = [None] * len(groups)
    for turn in range(ROUNDS):
        final = turn == ROUNDS - 1
        for k, group in enumerate(groups):
            if turn:
                wait_all(flight[k])
                for item, whole in zip(group.items, factors(group)):
                    kind, which = items[item]
                    kinds[kind][7][which] = jnp.concatenate(split(whole), axis=0)
            left_half(group, 1 - tp, group.send, 0, not turn)
            across = to_sibling(group, 0, group.send, group.inbox)
            left_half(group, tp, group.mine, 1, not turn)
            across.wait()
            used = group.inbox.shape[0]
            group.mine[0:used, :] += group.inbox[...]
            flight[k] = scatter(group, group.mine, group.land)
        for k, group in enumerate(groups):
            wait_all(flight[k])
            flight[k] = trade(group.mine, group.land, group.cross, group.x_send, group.x_recv)
        for k, group in enumerate(groups):
            wait_all(flight[k])
            flight[k] = gather(group, group.cross, group.panel.at[tp])
        for k, group in enumerate(groups):
            wait_all(flight[k])
            across = to_sibling(group, 1, group.panel.at[tp], group.panel.at[tp])
            right_half(group, tp, True)
            across.wait()
            right_half(group, 1 - tp, False)
            flight[k] = scatter(group, group.part, group.landq)
        for k, group in enumerate(groups):
            if k == 0:
                orthonormal(group, final)
            wait_all(flight[k])
            flight[k] = trade(group.part, group.landq, group.crossq, group.xq_send, group.xq_recv)
        for k, group in enumerate(groups):
            wait_all(flight[k])
            flight[k] = gather(group, group.crossq, group.total)
        for k, group in enumerate(groups):
            if k > 0:
                orthonormal(group, final)
    for k, group in enumerate(groups):
        wait_all(flight[k])
        base = (tp * all_blocks + first_block[group.items[0]]) * rank
        at = 0
        for item, whole in zip(group.items, factors(group)):
            for b in range(widths[item] // LANES):
                both[rows_at(base + at, rank), :] = whole[:, b * LANES : (b + 1) * LANES]
                at += rank
        view = both.at[rows_at(base, at)]
        flight[k] = to_sibling(group, 2, view, view)
    wait_all(flight + saves)


def last_kernel(rank, ortho, both, xs, xn, ms, mn, rs, rn, fs, fn, vs, vn, ks, kn, rows_s, rows_n):
    step = pl.program_id(0)
    widths = [xs.shape[2]] * xs.shape[0] + [xn.shape[2]] * xn.shape[0]
    first, blocks = first_blocks(widths)
    tp = lax.axis_index("tp")
    place = lax.axis_index("rep") * lax.axis_size("tp") + tp
    own = pl.multiple_of(tp * blocks * rank, blocks * rank)

    def wide(whole):
        hi, lo = split(whole)
        return jnp.concatenate([hi, hi, lo], axis=0)

    def tall(part):
        hi, lo = split(part)
        return jnp.concatenate([hi, lo, hi], axis=0)

    @pl.when(step == 0)
    def _():
        item = 0
        for f, k, m, v, rows_ref in ((fs, ks, ms, vs, rows_s), (fn, kn, mn, vn, rows_n)):
            per_row = rows_ref.shape[0]
            rows = m.shape[0] // (f.shape[0] * per_row)
            interleaved = f is fn
            at = place * rows
            block, inside = at // LANES, lax.rem(at, LANES)
            for which in range(f.shape[0]):
                width = widths[item]
                pieces = [
                    both[pl.ds(own + (first[item] + b) * rank, rank), :]
                    for b in range(width // LANES)
                ]
                mine = jnp.concatenate(pieces, axis=1)
                f[which] = mine
                k[which] = wide(mine)
                full = jnp.concatenate(
                    [factor_of(both, first[item], width, rank, core * blocks) for core in range(2)],
                    axis=1,
                )
                left = tall(ortho[block, item * rank : (item + 1) * rank, :])
                approx = dot(left, wide(full), TN)
                for c in range(per_row):
                    rows_ref[c] = approx[:, c * LANES : (c + 1) * LANES]
                for c in range(per_row):
                    if interleaved:
                        spot = pl.ds(c * f.shape[0] + which, rows, stride=per_row * f.shape[0])
                    else:
                        spot = pl.ds(which * rows * per_row + c, rows, stride=per_row)
                    v[spot, :] = (
                        momentum_decay * m[spot, :]
                        + rows_ref[c, pl.ds(pl.multiple_of(inside, 8), rows), :]
                    )
                item += 1

    per = BAND // LANES
    band = jnp.concatenate([ortho[step * per + b] for b in range(per)], axis=1)
    item = 0
    for x, k, r in ((xs, ks, rs), (xn, kn, rn)):
        for which in range(x.shape[0]):
            left = tall(band[item * rank : (item + 1) * rank])
            r[which] = x[which] - dot(left, k[which], TN)
            item += 1


def on_device(gn, en, sn, mn, gs, es, ss, ms):
    replicas = lax.axis_size("rep")
    shape_gn, shape_gs, shape_sn, shape_ss = gn.shape, gs.shape, sn.shape, ss.shape
    shape_mn, shape_ms = mn.shape, ms.shape
    gn, en, gs, es = (
        x.reshape((x.shape[1] * x.shape[2],) + x.shape[3:]) for x in (gn, en, gs, es)
    )
    sn, ss = (jnp.swapaxes(x.reshape((-1,) + x.shape[2:]), 1, 2) for x in (sn, ss))
    cn, depth, wn = gn.shape
    cs, _, ws = gs.shape
    rank = sn.shape[1]
    items = cn + cs
    steps, per, blocks = depth // BAND, BAND // LANES, depth // LANES
    widths = [ws] * cs + [wn] * cn
    _, all_blocks = first_blocks(widths)
    mn = jnp.swapaxes(mn.reshape(cn, -1, LANES), 0, 1).reshape(-1, LANES)
    ms = ms.reshape(-1, LANES)
    runs = groups_of(widths)

    in_vmem = pl.BlockSpec(memory_space=pltpu.VMEM)
    anywhere = pl.BlockSpec(memory_space=pl.ANY)

    def group_scratch(run):
        size = len(run) * rank
        half_rows, q_rows = blocks // 2 * size, sum(widths[i] for i in run) // LANES * rank
        near = near_size(replicas)
        far = replicas // near
        share, share_q = share_of(half_rows, near), share_of(q_rows, near)
        return [
            pltpu.VMEM((half_rows, LANES), f32),
            pltpu.VMEM((half_rows, LANES), f32),
            pltpu.VMEM((share * near, LANES), f32),
            pltpu.VMEM((2, share * near, LANES), f32),
            pltpu.VMEM((near - 1, share, LANES), f32),
            pltpu.VMEM((far, share, LANES), f32),
            pltpu.VMEM((share_q * near, LANES), f32),
            pltpu.VMEM((share_q * near, LANES), f32),
            pltpu.VMEM((near - 1, share_q, LANES), f32),
            pltpu.VMEM((far, share_q, LANES), f32),
            pltpu.VMEM((size, size), f32),
            pltpu.SemaphoreType.DMA((6,)),
        ] + [pltpu.SemaphoreType.DMA((count,)) for count in (near, near, near, near, far, far, far, far)]

    scratch = []
    for g, f in ((gs, ss), (gn, sn)):
        twice = (f.shape[0], 2 * rank, f.shape[2])
        scratch += [
            pltpu.VMEM(shape, kind)
            for shape, kind in (
                (g.shape, bf16), (g.shape, f32), (f.shape, f32), (g.shape, bf16), (g.shape, bf16), (twice, bf16)
            )
        ]
    scratch += [pltpu.SemaphoreType.DMA((n,)) for n in (4 * items, 2, 2 * items)]
    for run in runs:
        scratch += group_scratch(run)
    panel_shape = (blocks, items * rank, LANES)
    factor_shape = (2 * all_blocks * rank, LANES)
    xs, xn, ortho, both = pl.pallas_call(
        functools.partial(main_kernel, rank, replicas, runs),
        in_specs=[anywhere] * 6,
        out_specs=[anywhere, anywhere, in_vmem, in_vmem],
        out_shape=[pltpu.VMEM(shape, f32) for shape in (gs.shape, gn.shape, panel_shape, factor_shape)],
        scratch_shapes=scratch,
        compiler_params=pltpu.CompilerParams(
            collective_id=0, has_side_effects=True, vmem_limit_bytes=VMEM_LIMIT
        ),
        name="rounds",
    )(*(pltpu.with_memory_space_constraint(x, pltpu.HBM) for x in (gs, es, ss, gn, en, sn)))

    band_n = pl.BlockSpec((cn, BAND, wn), lambda t: (0, t, 0))
    band_s = pl.BlockSpec((cs, BAND, ws), lambda t: (0, t, 0))

    def full(shape):
        return pl.BlockSpec(shape, lambda t: (0,) * len(shape))

    rs, rn, fs, fn, vs, vn = pl.pallas_call(
        functools.partial(last_kernel, rank),
        grid=(steps,),
        in_specs=[full(panel_shape), full(factor_shape)]
        + [band_s, band_n]
        + [full(ms.shape), full(mn.shape)],
        out_specs=[
            band_s, band_n, full(ss.shape), full(sn.shape), full(ms.shape), full(mn.shape),
        ],
        out_shape=[
            jax.ShapeDtypeStruct(x.shape, f32) for x in (gs, gn, ss, sn, ms, mn)
        ],
        scratch_shapes=[
            pltpu.VMEM((cs, 3 * rank, ws), bf16),
            pltpu.VMEM((cn, 3 * rank, wn), bf16),
            pltpu.VMEM((2 * ws // LANES, LANES, LANES), f32),
            pltpu.VMEM((2 * wn // LANES, LANES, LANES), f32),
        ],
        compiler_params=pltpu.CompilerParams(vmem_limit_bytes=LAST_LIMIT),
        name="last",
    )(ortho, both, xs, xn, ms, mn)
    return (
        rn.reshape(shape_gn),
        jnp.swapaxes(fn, 1, 2).reshape(shape_sn),
        jnp.swapaxes(vn.reshape(-1, cn, LANES), 0, 1).reshape(shape_mn),
        rs.reshape(shape_gs),
        jnp.swapaxes(fs, 1, 2).reshape(shape_ss),
        vs.reshape(shape_ms),
    )


def solution(mesh):
    in_specs = (
        P("rep", None, None, None, "tp"),
        P("rep", None, None, None, "tp"),
        P(None, None, "tp", None),
        P(None, None, ("rep", "tp")),
        P("rep", None, None, None, "tp"),
        P("rep", None, None, None, "tp"),
        P(None, None, "tp", None),
        P(None, None, ("rep", "tp")),
    )
    out_specs = (
        P("rep", None, None, None, "tp"),
        P(None, None, "tp", None),
        P(None, None, ("rep", "tp")),
        P("rep", None, None, None, "tp"),
        P(None, None, "tp", None),
        P(None, None, ("rep", "tp")),
    )
    return jax.shard_map(
        on_device, mesh=mesh, in_specs=in_specs, out_specs=out_specs, check_vma=False
    )
```

```python
import functools

import jax
import jax.numpy as jnp
from jax import lax
from jax.experimental import pallas as pl
from jax.experimental.pallas import tpu as pltpu
from jax.sharding import PartitionSpec as P

ROUNDS = 2
NS_STEPS = 5
LANES = 128
BAND = 256
NEAR = 8
AHEAD = 3
VMEM_LIMIT = 40 * 1024 * 1024
LAST_LIMIT = 24 * 1024 * 1024

epsilon = 1e-06
momentum_decay = 0.9
highest = lax.Precision.HIGHEST
f32, bf16 = jnp.float32, jnp.bfloat16
MESH = pl.DeviceIdType.MESH


def split(x):
    hi = x.astype(bf16)
    lo = (x - hi.astype(f32)).astype(bf16)
    return hi, lo


def dot(a, b, dims, precision=None):
    return lax.dot_general(a, b, (dims, ((), ())), precision=precision, preferred_element_type=f32)


NN, NT, TN = ((1,), (0,)), ((1,), (1,)), ((0,), (0,))


def rows_at(at, size, unit=8):
    return pl.ds(pl.multiple_of(at, unit), size)


def first_blocks(widths):
    first, at = [], 0
    for width in widths:
        first.append(at)
        at += width // LANES
    return first, at


def factor_of(ref, first, width, rank, offset=0):
    pieces = [
        ref[(offset + first + b) * rank : (offset + first + b + 1) * rank, :]
        for b in range(width // LANES)
    ]
    return jnp.concatenate(pieces, axis=1)


def items_of(square, narrow):
    return [(0, which) for which in range(square)] + [(1, which) for which in range(narrow)]


SPLITS = 2


def groups_of(widths):
    half, total, cut = sum(widths) / 2, 0, len(widths)
    for at, width in enumerate(widths):
        if total >= half:
            cut = at
            break
        total += width
    runs = []
    for team, (start, stop) in enumerate(((0, cut), (cut, len(widths)))):
        count = min(SPLITS, stop - start)
        for part in range(count):
            first = start + part * (stop - start) // count
            last = start + (part + 1) * (stop - start) // count
            runs.append((range(first, last), team))
    return runs


def share_of(rows, parts):
    return -(-rows // (8 * parts)) * 8


def near_size(replicas):
    return NEAR if replicas % NEAR == 0 else replicas


class Group:
    names = (
        "send", "inbox", "mine", "panel", "land", "cross", "part", "total", "landq", "crossq", "turn",
        "side_left", "side_panel", "side_factor", "step_scatter", "step_trade", "step_gather",
        "step_scatter_q", "step_trade_q", "step_gather_q",
    )

    def __init__(self, items, team, refs):
        self.items, self.team = items, team
        for name, ref in zip(self.names, refs):
            setattr(self, name, ref)


def main_kernel(rank, replicas, runs, *refs):
    gs, es, ss, gn, en, sn, out_s, out_n, ortho, both = refs[:10]
    stage_gs, stage_es, stage_ss, hs, ls, fs, stage_gn, stage_en, stage_sn, hn, ln, fn = refs[10:22]
    load_sem, start_sem, save_sem = refs[22:25]
    per = len(Group.names)
    groups = [
        Group(run, team, refs[25 + per * k : 25 + per * (k + 1)]) for k, (run, team) in enumerate(runs)
    ]
    rep, tp = lax.axis_index("rep"), lax.axis_index("tp")
    other = {"rep": rep, "tp": 1 - tp}
    part = hs.shape[1] // 2
    blocks = part // LANES
    kinds = (
        (gs, es, stage_ss, hs, ls, stage_gs, stage_es, fs),
        (gn, en, stage_sn, hn, ln, stage_gn, stage_en, fn),
    )
    items = items_of(hs.shape[0], hn.shape[0])
    widths = [kinds[kind][3].shape[2] for kind, _ in items]
    first_block, all_blocks = first_blocks(widths)

    near = near_size(replicas)
    far = replicas // near
    near_at, far_at = lax.rem(rep, near), rep // near
    near_order = sorted(range(1, near), key=lambda j: -bin(j).count("1"))

    def near_of(j):
        result, bit = 0, 1
        while bit < near:
            here = lax.rem(near_at // bit, 2)
            result = result + bit * (1 - here if j & bit else here)
            bit *= 2
        return result

    def near_peer(j):
        return {"rep": far_at * near + near_of(j), "tp": tp}

    def far_peer(j):
        return {"rep": lax.rem(far_at + j, far) * near + near_at, "tp": tp}

    barrier = pltpu.get_barrier_semaphore()

    partners = [near_peer(j) for j in near_order] + [far_peer(j) for j in range(1, far)] + [other]
    for partner in partners:
        pl.semaphore_signal(barrier, inc=1, device_id=partner, device_id_type=MESH)

    starts = [
        pltpu.make_async_copy(src, dst, start_sem.at[i])
        for i, (src, dst) in enumerate(((ss, stage_ss), (sn, stage_sn)))
    ]
    for copy in starts:
        copy.start()
    def wait_all(copies):
        for copy in copies:
            copy.wait()

    loads, saves = [], []
    for where, half in enumerate((1 - tp, tp)):
        rows = rows_at(half * part, part, LANES)
        for group in groups:
            for item in group.items:
                kind, which = items[item]
                g, e, _, _, _, sg, se, _ = kinds[kind]
                pair = []
                for src, dst in ((g, sg), (e, se)):
                    at = 2 * len(loads) + len(pair)
                    pair.append(
                        pltpu.make_async_copy(src.at[which, rows], dst.at[which, rows], load_sem.at[at])
                    )
                loads.append(pair)
    for pair in loads[:AHEAD]:
        for copy in pair:
            copy.start()
    used = [0]

    def next_load():
        at = used[0]
        used[0] += 1
        for copy in loads[at + AHEAD : at + AHEAD + 1]:
            for one in copy:
                one.start()
        wait_all(loads[at])

    for copy in starts:
        copy.wait()
    for kind, which in items:
        start, keep = kinds[kind][2], kinds[kind][7]
        keep[which] = jnp.concatenate(split(start[which]), axis=0)

    class Flight:
        def __init__(self, slot, all_bytes):
            self.slot, self.all_bytes, self.sent = slot, all_bytes, True

        def wait(self, side):
            pltpu.make_async_copy(self.all_bytes, self.all_bytes, self.slot.at[side]).wait()

    def spread(order, source, target, slot, all_bytes, to):
        for j in order:
            pltpu.make_async_remote_copy(
                src_ref=source(j), dst_ref=target(j), send_sem=slot.at[0], recv_sem=slot.at[1],
                device_id=to(j), device_id_type=MESH,
            ).start()
        return Flight(slot, all_bytes)

    unsent = {}

    def depart(name, flight):
        unsent[name] = flight
        return flight

    def reuse(*names):
        for name in names:
            if name in unsent:
                unsent.pop(name).wait(0)

    def scatter(group, mine, land, slot):
        share = land.shape[1]
        return spread(
            near_order, lambda j: mine.at[rows_at(near_of(j) * share, share)], lambda j: land.at[j - 1],
            slot, land, near_peer,
        )

    def trade(mine, land, cross, slot):
        share = land.shape[1]
        own = rows_at(near_at * share, share)
        value = mine[own, :]
        for j in range(near - 1):
            value = value + land[j]
        cross[far_at] = value
        view = cross.at[far_at]
        return spread(range(1, far), lambda j: view, lambda j: view, slot, cross.at[0 : far - 1], far_peer)

    def gather(cross, whole, slot):
        share = cross.shape[1]
        own = rows_at(near_at * share, share)
        value = cross[0]
        for j in range(1, far):
            value = value + cross[j]
        whole[own, :] = value
        view = whole.at[own]
        return spread(
            near_order, lambda j: view, lambda j: view, slot, whole.at[0 : (near - 1) * share], near_peer
        )

    def to_sibling(src, dst, slot):
        return spread((0,), lambda j: src, lambda j: dst, slot, src, lambda j: other)

    def left_half(group, half, out, fresh):
        size = len(group.items) * rank
        for place, item in enumerate(group.items):
            kind, which = items[item]
            _, _, _, h, l, sg, se, keep = kinds[kind]
            if fresh:
                next_load()
            stacked = keep[which]
            for band in range(part // BAND):
                rows = rows_at(half * part + band * BAND, BAND, LANES)
                if fresh:
                    merged = sg[which, rows, :].astype(f32) + se[which, rows, :]
                    hi, lo = split(merged)
                    se[which, rows, :], h[which, rows, :], l[which, rows, :] = merged, hi, lo
                else:
                    hi, lo = h[which, rows, :], l[which, rows, :]
                twice = dot(stacked, hi, NT)
                result = twice[:rank] + twice[rank:] + dot(stacked[:rank], lo, NT)
                for b in range(BAND // LANES):
                    at = (band * (BAND // LANES) + b) * size + place * rank
                    out[at : at + rank, :] = result[:, b * LANES : (b + 1) * LANES]
            if fresh:
                rows = rows_at(half * part, part, LANES)
                target = (out_s, out_n)[kind]
                copy = pltpu.make_async_copy(se.at[which, rows], target.at[which, rows], save_sem.at[len(saves)])
                copy.start()
                saves.append(copy)

    def panel_half(group, half):
        size = len(group.items) * rank
        return [group.panel[half, b * size : (b + 1) * size, :] for b in range(blocks)]

    def right_half(group, half, first):
        wide = jnp.concatenate(panel_half(group, half), axis=1)
        rows = rows_at(half * part, part, LANES)
        at = 0
        for place, item in enumerate(group.items):
            kind, which = items[item]
            h, l = kinds[kind][3:5]
            hi, lo = split(wide[place * rank : (place + 1) * rank])
            twice = dot(jnp.concatenate([hi, lo], axis=0), h[which, rows, :], NN)
            term = twice[:rank] + twice[rank:] + dot(hi, l[which, rows, :], NN)
            for b in range(widths[item] // LANES):
                piece = term[:, b * LANES : (b + 1) * LANES]
                if first:
                    group.part[at : at + rank, :] = piece
                else:
                    group.part[at : at + rank, :] += piece
                at += rank

    def orthonormal(team, final):
        sizes = [len(group.items) * rank for group in team]
        size = sum(sizes)
        stacked = jnp.concatenate(
            [jnp.concatenate(panel_half(group, 0) + panel_half(group, 1), axis=1) for group in team], axis=0
        )
        row = lax.broadcasted_iota(jnp.int32, (size, size), 0)
        column = lax.broadcasted_iota(jnp.int32, (size, size), 1)
        own = (row // rank) == (column // rank)
        identity = jnp.where(row == column, 1.0, 0.0).astype(f32)
        scale, scaled = [], []
        for place in range(size // rank):
            piece = stacked[place * rank : (place + 1) * rank]
            by = 1.0 / (jnp.sqrt(jnp.sum(piece * piece)) + epsilon)
            scale.append(jnp.full((rank, size), by, f32))
            scaled.append(piece * by)
        scaled = jnp.concatenate(scaled, axis=0)
        gram = jnp.where(own, dot(scaled, scaled, NT, highest), 0.0)
        total = None
        for sweep in range(NS_STEPS):
            turn = 1.5 * identity - 0.5 * gram
            total = turn if total is None else dot(turn, total, NN, highest)
            if sweep < NS_STEPS - 1:
                gram = dot(dot(turn, gram, NN, highest), turn, NN, highest)
        result = dot(total, scaled, NN, highest) if final else None
        total = total * jnp.concatenate(scale, axis=0)
        at = 0
        for group, width in zip(team, sizes):
            group.turn[...] = total[at : at + width, at : at + width]
            if final:
                base = group.items[0] * rank
                for b in range(2 * blocks):
                    ortho[b, base : base + width, :] = result[at : at + width, b * LANES : (b + 1) * LANES]
            at += width

    def factors(group):
        at, result = 0, []
        for place, item in enumerate(group.items):
            own = slice(place * rank, (place + 1) * rank)
            pieces = []
            for b in range(widths[item] // LANES):
                pieces.append(group.total[at : at + rank, :])
                at += rank
            turned = dot(group.turn[own, own] / replicas, jnp.concatenate(pieces, axis=1), NN, highest)
            result.append(turned)
        return result

    flight = [None] * len(groups)
    teams = [[k for k, group in enumerate(groups) if group.team == team] for team in range(2)]
    for turn in range(ROUNDS):
        final = turn == ROUNDS - 1
        across = []
        for k, group in enumerate(groups):
            if turn:
                flight[k].wait(1)
                for item, whole in zip(group.items, factors(group)):
                    kind, which = items[item]
                    kinds[kind][7][which] = jnp.concatenate(split(whole), axis=0)
            reuse((k, "left"), (k, "side"))
            left_half(group, 1 - tp, group.send, not turn)
            if not turn and k == 0:
                pl.semaphore_wait(barrier, len(partners))
            across.append(depart((k, "left"), to_sibling(group.send, group.inbox, group.side_left)))
        for k, group in enumerate(groups):
            reuse((k, "scatter"))
            left_half(group, tp, group.mine, not turn)
            across[k].wait(1)
            used_rows = group.inbox.shape[0]
            group.mine[0:used_rows, :] += group.inbox[...]
            flight[k] = depart((k, "scatter"), scatter(group, group.mine, group.land, group.step_scatter))
        for k, group in enumerate(groups):
            flight[k].wait(1)
            reuse((k, "trade"))
            flight[k] = depart((k, "trade"), trade(group.mine, group.land, group.cross, group.step_trade))
        for k, group in enumerate(groups):
            flight[k].wait(1)
            reuse((k, "gather"))
            flight[k] = depart((k, "gather"), gather(group.cross, group.panel.at[tp], group.step_gather))
        across = []
        for k, group in enumerate(groups):
            flight[k].wait(1)
            view = group.panel.at[tp]
            across.append(depart((k, "side"), to_sibling(view, view, group.side_panel)))
            reuse((k, "scatter_q"))
            right_half(group, tp, True)
        for k, group in enumerate(groups):
            across[k].wait(1)
            right_half(group, 1 - tp, False)
            flight[k] = depart((k, "scatter_q"), scatter(group, group.part, group.landq, group.step_scatter_q))
        orthonormal([groups[k] for k in teams[0]], final)
        for k, group in enumerate(groups):
            flight[k].wait(1)
            reuse((k, "trade_q"))
            flight[k] = depart((k, "trade_q"), trade(group.part, group.landq, group.crossq, group.step_trade_q))
        for k, group in enumerate(groups):
            flight[k].wait(1)
            reuse((k, "gather_q"))
            flight[k] = depart((k, "gather_q"), gather(group.crossq, group.total, group.step_gather_q))
        if teams[1]:
            orthonormal([groups[k] for k in teams[1]], final)
    for k, group in enumerate(groups):
        flight[k].wait(1)
        base = (tp * all_blocks + first_block[group.items[0]]) * rank
        at = 0
        for item, whole in zip(group.items, factors(group)):
            for b in range(widths[item] // LANES):
                both[rows_at(base + at, rank), :] = whole[:, b * LANES : (b + 1) * LANES]
                at += rank
        view = both.at[rows_at(base, at)]
        flight[k] = depart((k, "factor"), to_sibling(view, view, group.side_factor))
    for last in flight:
        last.wait(1)
    reuse(*list(unsent))
    wait_all(saves)


def last_kernel(
    rank, ortho, both, xs, xn, ms, mn, rs, rn, fs, fn, vs, vn,
    ks, kn, rows_s, rows_n, res_s, res_n, fac_s, fac_n, vel_s, vel_n, sem,
):
    widths = [xs.shape[2]] * xs.shape[0] + [xn.shape[2]] * xn.shape[0]
    first, blocks = first_blocks(widths)
    tp = lax.axis_index("tp")
    place = lax.axis_index("rep") * lax.axis_size("tp") + tp
    own = pl.multiple_of(tp * blocks * rank, blocks * rank)
    started = []

    def out(src, dst):
        copy = pltpu.make_async_copy(src, dst, sem.at[len(started)])
        copy.start()
        started.append(copy)

    def wide(whole):
        hi, lo = split(whole)
        return jnp.concatenate([hi, hi, lo], axis=0)

    def tall(part):
        hi, lo = split(part)
        return jnp.concatenate([hi, lo, hi], axis=0)

    def residue(step):
        per = BAND // LANES
        rows = slice(step * BAND, (step + 1) * BAND)
        band = jnp.concatenate([ortho[step * per + b] for b in range(per)], axis=1)
        item = 0
        for x, k, kept, r in ((xs, ks, res_s, rs), (xn, kn, res_n, rn)):
            for which in range(x.shape[0]):
                if step == 0:
                    pieces = [
                        both[pl.ds(own + (first[item] + b) * rank, rank), :]
                        for b in range(widths[item] // LANES)
                    ]
                    mine = jnp.concatenate(pieces, axis=1)
                    (fac_s if x is xs else fac_n)[which] = mine
                    k[which] = wide(mine)
                left = tall(band[item * rank : (item + 1) * rank])
                kept[which, rows] = x[which, rows] - dot(left, k[which], TN)
                out(kept.at[which, rows], r.at[which, rows])
                item += 1

    def velocity():
        item = 0
        for f, m, v, rows_ref in ((fac_s, ms, vel_s, rows_s), (fac_n, mn, vel_n, rows_n)):
            per_row = rows_ref.shape[0]
            rows = m.shape[0] // (f.shape[0] * per_row)
            interleaved = f is fac_n
            at = place * rows
            block, inside = at // LANES, lax.rem(at, LANES)
            for which in range(f.shape[0]):
                full = jnp.concatenate(
                    [factor_of(both, first[item], widths[item], rank, core * blocks) for core in range(2)],
                    axis=1,
                )
                left = tall(ortho[block, item * rank : (item + 1) * rank, :])
                approx = dot(left, wide(full), TN)
                for c in range(per_row):
                    rows_ref[c] = approx[:, c * LANES : (c + 1) * LANES]
                for c in range(per_row):
                    if interleaved:
                        spot = pl.ds(c * f.shape[0] + which, rows, stride=per_row * f.shape[0])
                    else:
                        spot = pl.ds(which * rows * per_row + c, rows, stride=per_row)
                    v[spot, :] = (
                        momentum_decay * m[spot, :]
                        + rows_ref[c, pl.ds(pl.multiple_of(inside, 8), rows), :]
                    )
                item += 1

    steps = xs.shape[1] // BAND
    for step in range(steps):
        residue(step)
        if step == steps - 2:
            velocity()
            for src, dst in ((fac_s, fs), (fac_n, fn), (vel_s, vs), (vel_n, vn)):
                out(src, dst)
    for copy in started:
        copy.wait()


def on_device(gn, en, sn, mn, gs, es, ss, ms):
    replicas = lax.axis_size("rep")
    shape_gn, shape_gs, shape_sn, shape_ss = gn.shape, gs.shape, sn.shape, ss.shape
    shape_mn, shape_ms = mn.shape, ms.shape
    gn, en, gs, es = (
        x.reshape((x.shape[1] * x.shape[2],) + x.shape[3:]) for x in (gn, en, gs, es)
    )
    sn, ss = (jnp.swapaxes(x.reshape((-1,) + x.shape[2:]), 1, 2) for x in (sn, ss))
    cn, depth, wn = gn.shape
    cs, _, ws = gs.shape
    rank = sn.shape[1]
    items = cn + cs
    blocks = depth // LANES
    widths = [ws] * cs + [wn] * cn
    _, all_blocks = first_blocks(widths)
    mn = jnp.swapaxes(mn.reshape(cn, -1, LANES), 0, 1).reshape(-1, LANES)
    ms = ms.reshape(-1, LANES)
    runs = groups_of(widths)

    in_vmem = pl.BlockSpec(memory_space=pltpu.VMEM)
    anywhere = pl.BlockSpec(memory_space=pl.ANY)

    def group_scratch(run):
        size = len(run) * rank
        half_rows, q_rows = blocks // 2 * size, sum(widths[i] for i in run) // LANES * rank
        near = near_size(replicas)
        far = replicas // near
        share, share_q = share_of(half_rows, near), share_of(q_rows, near)
        return [
            pltpu.VMEM((half_rows, LANES), f32),
            pltpu.VMEM((half_rows, LANES), f32),
            pltpu.VMEM((share * near, LANES), f32),
            pltpu.VMEM((2, share * near, LANES), f32),
            pltpu.VMEM((near - 1, share, LANES), f32),
            pltpu.VMEM((far, share, LANES), f32),
            pltpu.VMEM((share_q * near, LANES), f32),
            pltpu.VMEM((share_q * near, LANES), f32),
            pltpu.VMEM((near - 1, share_q, LANES), f32),
            pltpu.VMEM((far, share_q, LANES), f32),
            pltpu.VMEM((size, size), f32),
        ] + [pltpu.SemaphoreType.DMA((2,)) for _ in range(9)]

    scratch = []
    for g, f in ((gs, ss), (gn, sn)):
        twice = (f.shape[0], 2 * rank, f.shape[2])
        scratch += [
            pltpu.VMEM(shape, kind)
            for shape, kind in (
                (g.shape, bf16), (g.shape, f32), (f.shape, f32), (g.shape, bf16), (g.shape, bf16), (twice, bf16)
            )
        ]
    scratch += [pltpu.SemaphoreType.DMA((n,)) for n in (4 * items, 2, 2 * items)]
    for run, _ in runs:
        scratch += group_scratch(run)
    panel_shape = (blocks, items * rank, LANES)
    factor_shape = (2 * all_blocks * rank, LANES)
    xs, xn, ortho, both = pl.pallas_call(
        functools.partial(main_kernel, rank, replicas, runs),
        in_specs=[anywhere] * 6,
        out_specs=[anywhere, anywhere, in_vmem, in_vmem],
        out_shape=[pltpu.VMEM(shape, f32) for shape in (gs.shape, gn.shape, panel_shape, factor_shape)],
        scratch_shapes=scratch,
        compiler_params=pltpu.CompilerParams(
            collective_id=0, has_side_effects=True, vmem_limit_bytes=VMEM_LIMIT
        ),
        name="rounds",
    )(*(pltpu.with_memory_space_constraint(x, pltpu.HBM) for x in (gs, es, ss, gn, en, sn)))

    results = [gs.shape, gn.shape, ss.shape, sn.shape, ms.shape, mn.shape]
    rs, rn, fs, fn, vs, vn = pl.pallas_call(
        functools.partial(last_kernel, rank),
        in_specs=[in_vmem] * 6,
        out_specs=[anywhere] * 6,
        out_shape=[jax.ShapeDtypeStruct(shape, f32) for shape in results],
        scratch_shapes=[
            pltpu.VMEM((cs, 3 * rank, ws), bf16),
            pltpu.VMEM((cn, 3 * rank, wn), bf16),
            pltpu.VMEM((2 * ws // LANES, LANES, LANES), f32),
            pltpu.VMEM((2 * wn // LANES, LANES, LANES), f32),
        ]
        + [pltpu.VMEM(shape, f32) for shape in results]
        + [pltpu.SemaphoreType.DMA((items * (depth // BAND) + 4,))],
        compiler_params=pltpu.CompilerParams(vmem_limit_bytes=LAST_LIMIT),
        name="last",
    )(ortho, both, xs, xn, ms, mn)
    return (
        rn.reshape(shape_gn),
        jnp.swapaxes(fn, 1, 2).reshape(shape_sn),
        jnp.swapaxes(vn.reshape(-1, cn, LANES), 0, 1).reshape(shape_mn),
        rs.reshape(shape_gs),
        jnp.swapaxes(fs, 1, 2).reshape(shape_ss),
        vs.reshape(shape_ms),
    )


def solution(mesh):
    in_specs = (
        P("rep", None, None, None, "tp"),
        P("rep", None, None, None, "tp"),
        P(None, None, "tp", None),
        P(None, None, ("rep", "tp")),
        P("rep", None, None, None, "tp"),
        P("rep", None, None, None, "tp"),
        P(None, None, "tp", None),
        P(None, None, ("rep", "tp")),
    )
    out_specs = (
        P("rep", None, None, None, "tp"),
        P(None, None, "tp", None),
        P(None, None, ("rep", "tp")),
        P("rep", None, None, None, "tp"),
        P(None, None, "tp", None),
        P(None, None, ("rep", "tp")),
    )
    return jax.shard_map(
        on_device, mesh=mesh, in_specs=in_specs, out_specs=out_specs, check_vma=False
    )
```

```python
import functools

import jax
import jax.numpy as jnp
from jax import lax
from jax.experimental import pallas as pl
from jax.experimental.pallas import tpu as pltpu
from jax.sharding import PartitionSpec as P

ROUNDS = 2
NS_STEPS = 5
LANES = 128
BAND = 256
NEAR = 8
AHEAD = 3
VMEM_LIMIT = 40 * 1024 * 1024
LAST_LIMIT = 24 * 1024 * 1024

epsilon = 1e-06
momentum_decay = 0.9
f32, bf16 = jnp.float32, jnp.bfloat16
MESH = pl.DeviceIdType.MESH


def split(x):
    hi = x.astype(bf16)
    lo = (x - hi.astype(f32)).astype(bf16)
    return hi, lo


def dot(a, b, dims):
    return lax.dot_general(a, b, (dims, ((), ())), preferred_element_type=f32)


NN, NT, TN = ((1,), (0,)), ((1,), (1,)), ((0,), (0,))


def dot3(a, b, dims=NN):
    (ah, al), (bh, bl) = split(a), split(b)
    return dot(ah, bh, dims) + (dot(ah, bl, dims) + dot(al, bh, dims))


def rows_at(at, size, unit=8):
    return pl.ds(pl.multiple_of(at, unit), size)


def first_blocks(widths):
    first, at = [], 0
    for width in widths:
        first.append(at)
        at += width // LANES
    return first, at


def factor_of(ref, first, width, rank, offset=0):
    pieces = [
        ref[(offset + first + b) * rank : (offset + first + b + 1) * rank, :]
        for b in range(width // LANES)
    ]
    return jnp.concatenate(pieces, axis=1)


def items_of(square, narrow):
    return [(0, which) for which in range(square)] + [(1, which) for which in range(narrow)]


SPLITS = 2


def groups_of(widths):
    half, total, cut = sum(widths) / 2, 0, len(widths)
    for at, width in enumerate(widths):
        if total >= half:
            cut = at
            break
        total += width
    runs = []
    for team, (start, stop) in enumerate(((0, cut), (cut, len(widths)))):
        count = min(SPLITS, stop - start)
        for part in range(count):
            first = start + part * (stop - start) // count
            last = start + (part + 1) * (stop - start) // count
            runs.append((range(first, last), team))
    return runs


def share_of(rows, parts):
    return -(-rows // (8 * parts)) * 8


def near_size(replicas):
    return NEAR if replicas % NEAR == 0 else replicas


class Group:
    names = (
        "send", "inbox", "mine", "panel", "land", "cross", "part", "total", "landq", "crossq", "turn",
        "side_left", "side_panel", "side_factor", "step_scatter", "step_trade", "step_gather",
        "step_scatter_q", "step_trade_q", "step_gather_q",
    )

    def __init__(self, items, team, refs):
        self.items, self.team = items, team
        for name, ref in zip(self.names, refs):
            setattr(self, name, ref)


def main_kernel(rank, replicas, runs, *refs):
    gs, es, ss, gn, en, sn, out_s, out_n, ortho, both = refs[:10]
    stage_gs, stage_es, stage_ss, hs, ls, fs, stage_gn, stage_en, stage_sn, hn, ln, fn = refs[10:22]
    load_sem, start_sem, save_sem = refs[22:25]
    per = len(Group.names)
    groups = [
        Group(run, team, refs[25 + per * k : 25 + per * (k + 1)]) for k, (run, team) in enumerate(runs)
    ]
    rep, tp = lax.axis_index("rep"), lax.axis_index("tp")
    other = {"rep": rep, "tp": 1 - tp}
    part = hs.shape[1] // 2
    blocks = part // LANES
    kinds = (
        (gs, es, stage_ss, hs, ls, stage_gs, stage_es, fs),
        (gn, en, stage_sn, hn, ln, stage_gn, stage_en, fn),
    )
    items = items_of(hs.shape[0], hn.shape[0])
    widths = [kinds[kind][3].shape[2] for kind, _ in items]
    first_block, all_blocks = first_blocks(widths)

    near = near_size(replicas)
    far = replicas // near
    near_at, far_at = lax.rem(rep, near), rep // near
    near_order = sorted(range(1, near), key=lambda j: -bin(j).count("1"))

    def near_of(j):
        result, bit = 0, 1
        while bit < near:
            here = lax.rem(near_at // bit, 2)
            result = result + bit * (1 - here if j & bit else here)
            bit *= 2
        return result

    def near_peer(j):
        return {"rep": far_at * near + near_of(j), "tp": tp}

    def far_peer(j):
        return {"rep": lax.rem(far_at + j, far) * near + near_at, "tp": tp}

    barrier = pltpu.get_barrier_semaphore()

    partners = [near_peer(j) for j in near_order] + [far_peer(j) for j in range(1, far)] + [other]
    for partner in partners:
        pl.semaphore_signal(barrier, inc=1, device_id=partner, device_id_type=MESH)

    starts = [
        pltpu.make_async_copy(src, dst, start_sem.at[i])
        for i, (src, dst) in enumerate(((ss, stage_ss), (sn, stage_sn)))
    ]
    for copy in starts:
        copy.start()
    def wait_all(copies):
        for copy in copies:
            copy.wait()

    loads, saves = [], []
    for where, half in enumerate((1 - tp, tp)):
        rows = rows_at(half * part, part, LANES)
        for group in groups:
            for item in group.items:
                kind, which = items[item]
                g, e, _, _, _, sg, se, _ = kinds[kind]
                pair = []
                for src, dst in ((g, sg), (e, se)):
                    at = 2 * len(loads) + len(pair)
                    pair.append(
                        pltpu.make_async_copy(src.at[which, rows], dst.at[which, rows], load_sem.at[at])
                    )
                loads.append(pair)
    for pair in loads[:AHEAD]:
        for copy in pair:
            copy.start()
    used = [0]

    def next_load():
        at = used[0]
        used[0] += 1
        for copy in loads[at + AHEAD : at + AHEAD + 1]:
            for one in copy:
                one.start()
        wait_all(loads[at])

    for copy in starts:
        copy.wait()
    for kind, which in items:
        start, keep = kinds[kind][2], kinds[kind][7]
        keep[which] = jnp.concatenate(split(start[which]), axis=0)

    class Flight:
        def __init__(self, slot, all_bytes):
            self.slot, self.all_bytes, self.sent = slot, all_bytes, True

        def wait(self, side):
            pltpu.make_async_copy(self.all_bytes, self.all_bytes, self.slot.at[side]).wait()

    def spread(order, source, target, slot, all_bytes, to):
        for j in order:
            pltpu.make_async_remote_copy(
                src_ref=source(j), dst_ref=target(j), send_sem=slot.at[0], recv_sem=slot.at[1],
                device_id=to(j), device_id_type=MESH,
            ).start()
        return Flight(slot, all_bytes)

    unsent = {}

    def depart(name, flight):
        unsent[name] = flight
        return flight

    def reuse(*names):
        for name in names:
            if name in unsent:
                unsent.pop(name).wait(0)

    def scatter(group, mine, land, slot):
        share = land.shape[1]
        return spread(
            near_order, lambda j: mine.at[rows_at(near_of(j) * share, share)], lambda j: land.at[j - 1],
            slot, land, near_peer,
        )

    def trade(mine, land, cross, slot):
        share = land.shape[1]
        own = rows_at(near_at * share, share)
        value = mine[own, :]
        for j in range(near - 1):
            value = value + land[j]
        cross[far_at] = value
        view = cross.at[far_at]
        return spread(range(1, far), lambda j: view, lambda j: view, slot, cross.at[0 : far - 1], far_peer)

    def gather(cross, whole, slot):
        share = cross.shape[1]
        own = rows_at(near_at * share, share)
        value = cross[0]
        for j in range(1, far):
            value = value + cross[j]
        whole[own, :] = value
        view = whole.at[own]
        return spread(
            near_order, lambda j: view, lambda j: view, slot, whole.at[0 : (near - 1) * share], near_peer
        )

    def to_sibling(src, dst, slot):
        return spread((0,), lambda j: src, lambda j: dst, slot, src, lambda j: other)

    def left_half(group, half, out, fresh):
        size = len(group.items) * rank
        for place, item in enumerate(group.items):
            kind, which = items[item]
            _, _, _, h, l, sg, se, keep = kinds[kind]
            if fresh:
                next_load()
            stacked = keep[which]
            for band in range(part // BAND):
                rows = rows_at(half * part + band * BAND, BAND, LANES)
                if fresh:
                    merged = sg[which, rows, :].astype(f32) + se[which, rows, :]
                    hi, lo = split(merged)
                    se[which, rows, :], h[which, rows, :], l[which, rows, :] = merged, hi, lo
                else:
                    hi, lo = h[which, rows, :], l[which, rows, :]
                twice = dot(stacked, hi, NT)
                result = twice[:rank] + twice[rank:] + dot(stacked[:rank], lo, NT)
                for b in range(BAND // LANES):
                    at = (band * (BAND // LANES) + b) * size + place * rank
                    out[at : at + rank, :] = result[:, b * LANES : (b + 1) * LANES]
            if fresh:
                rows = rows_at(half * part, part, LANES)
                target = (out_s, out_n)[kind]
                copy = pltpu.make_async_copy(se.at[which, rows], target.at[which, rows], save_sem.at[len(saves)])
                copy.start()
                saves.append(copy)

    def panel_half(group, half):
        size = len(group.items) * rank
        return [group.panel[half, b * size : (b + 1) * size, :] for b in range(blocks)]

    def right_half(group, half, first):
        wide = jnp.concatenate(panel_half(group, half), axis=1)
        rows = rows_at(half * part, part, LANES)
        at = 0
        for place, item in enumerate(group.items):
            kind, which = items[item]
            h, l = kinds[kind][3:5]
            hi, lo = split(wide[place * rank : (place + 1) * rank])
            twice = dot(jnp.concatenate([hi, lo], axis=0), h[which, rows, :], NN)
            term = twice[:rank] + twice[rank:] + dot(hi, l[which, rows, :], NN)
            for b in range(widths[item] // LANES):
                piece = term[:, b * LANES : (b + 1) * LANES]
                if first:
                    group.part[at : at + rank, :] = piece
                else:
                    group.part[at : at + rank, :] += piece
                at += rank

    def orthonormal(team, final):
        sizes = [len(group.items) * rank for group in team]
        size = sum(sizes)
        stacked = jnp.concatenate(
            [jnp.concatenate(panel_half(group, 0) + panel_half(group, 1), axis=1) for group in team], axis=0
        )
        row = lax.broadcasted_iota(jnp.int32, (size, size), 0)
        column = lax.broadcasted_iota(jnp.int32, (size, size), 1)
        own = (row // rank) == (column // rank)
        identity = jnp.where(row == column, 1.0, 0.0).astype(f32)
        scale, scaled = [], []
        for place in range(size // rank):
            piece = stacked[place * rank : (place + 1) * rank]
            by = 1.0 / (jnp.sqrt(jnp.sum(piece * piece)) + epsilon)
            scale.append(jnp.full((rank, size), by, f32))
            scaled.append(piece * by)
        scaled = jnp.concatenate(scaled, axis=0)
        gram = jnp.where(own, dot3(scaled, scaled, NT), 0.0)
        total = None
        for sweep in range(NS_STEPS):
            turn = 1.5 * identity - 0.5 * gram
            total = turn if total is None else dot3(turn, total)
            if sweep < NS_STEPS - 1:
                gram = dot3(dot3(turn, gram), turn)
        result = dot3(total, scaled) if final else None
        total = total * jnp.concatenate(scale, axis=0)
        at = 0
        for group, width in zip(team, sizes):
            group.turn[...] = total[at : at + width, at : at + width]
            if final:
                base = group.items[0] * rank
                for b in range(2 * blocks):
                    ortho[b, base : base + width, :] = result[at : at + width, b * LANES : (b + 1) * LANES]
            at += width

    def factors(group):
        at, result = 0, []
        for place, item in enumerate(group.items):
            own = slice(place * rank, (place + 1) * rank)
            pieces = []
            for b in range(widths[item] // LANES):
                pieces.append(group.total[at : at + rank, :])
                at += rank
            turned = dot3(group.turn[own, own] / replicas, jnp.concatenate(pieces, axis=1))
            result.append(turned)
        return result

    flight = [None] * len(groups)
    teams = [[k for k, group in enumerate(groups) if group.team == team] for team in range(2)]
    for turn in range(ROUNDS):
        final = turn == ROUNDS - 1
        across = []
        for k, group in enumerate(groups):
            if turn:
                flight[k].wait(1)
                for item, whole in zip(group.items, factors(group)):
                    kind, which = items[item]
                    kinds[kind][7][which] = jnp.concatenate(split(whole), axis=0)
            reuse((k, "left"), (k, "side"))
            left_half(group, 1 - tp, group.send, not turn)
            if not turn and k == 0:
                pl.semaphore_wait(barrier, len(partners))
            across.append(depart((k, "left"), to_sibling(group.send, group.inbox, group.side_left)))
        for k, group in enumerate(groups):
            reuse((k, "scatter"))
            left_half(group, tp, group.mine, not turn)
            across[k].wait(1)
            used_rows = group.inbox.shape[0]
            group.mine[0:used_rows, :] += group.inbox[...]
            flight[k] = depart((k, "scatter"), scatter(group, group.mine, group.land, group.step_scatter))
        for k, group in enumerate(groups):
            flight[k].wait(1)
            reuse((k, "trade"))
            flight[k] = depart((k, "trade"), trade(group.mine, group.land, group.cross, group.step_trade))
        for k, group in enumerate(groups):
            flight[k].wait(1)
            reuse((k, "gather"))
            flight[k] = depart((k, "gather"), gather(group.cross, group.panel.at[tp], group.step_gather))
        across = []
        for k, group in enumerate(groups):
            flight[k].wait(1)
            view = group.panel.at[tp]
            across.append(depart((k, "side"), to_sibling(view, view, group.side_panel)))
            reuse((k, "scatter_q"))
            right_half(group, tp, True)
        for k, group in enumerate(groups):
            across[k].wait(1)
            right_half(group, 1 - tp, False)
            flight[k] = depart((k, "scatter_q"), scatter(group, group.part, group.landq, group.step_scatter_q))
        orthonormal([groups[k] for k in teams[0]], final)
        for k, group in enumerate(groups):
            flight[k].wait(1)
            reuse((k, "trade_q"))
            flight[k] = depart((k, "trade_q"), trade(group.part, group.landq, group.crossq, group.step_trade_q))
        for k, group in enumerate(groups):
            flight[k].wait(1)
            reuse((k, "gather_q"))
            flight[k] = depart((k, "gather_q"), gather(group.crossq, group.total, group.step_gather_q))
        if teams[1]:
            orthonormal([groups[k] for k in teams[1]], final)
    for k, group in enumerate(groups):
        flight[k].wait(1)
        base = (tp * all_blocks + first_block[group.items[0]]) * rank
        at = 0
        for item, whole in zip(group.items, factors(group)):
            for b in range(widths[item] // LANES):
                both[rows_at(base + at, rank), :] = whole[:, b * LANES : (b + 1) * LANES]
                at += rank
        view = both.at[rows_at(base, at)]
        flight[k] = depart((k, "factor"), to_sibling(view, view, group.side_factor))
    for last in flight:
        last.wait(1)
    reuse(*list(unsent))
    wait_all(saves)


def last_kernel(
    rank, ortho, both, xs, xn, ms, mn, rs, rn, fs, fn, vs, vn,
    ks, kn, rows_s, rows_n, res_s, res_n, fac_s, fac_n, vel_s, vel_n, sem,
):
    widths = [xs.shape[2]] * xs.shape[0] + [xn.shape[2]] * xn.shape[0]
    first, blocks = first_blocks(widths)
    tp = lax.axis_index("tp")
    place = lax.axis_index("rep") * lax.axis_size("tp") + tp
    own = pl.multiple_of(tp * blocks * rank, blocks * rank)
    started = []

    def out(src, dst):
        copy = pltpu.make_async_copy(src, dst, sem.at[len(started)])
        copy.start()
        started.append(copy)

    def wide(whole):
        hi, lo = split(whole)
        return jnp.concatenate([hi, hi, lo], axis=0)

    def tall(part):
        hi, lo = split(part)
        return jnp.concatenate([hi, lo, hi], axis=0)

    def residue(step):
        per = BAND // LANES
        rows = slice(step * BAND, (step + 1) * BAND)
        band = jnp.concatenate([ortho[step * per + b] for b in range(per)], axis=1)
        item = 0
        for x, k, kept, r in ((xs, ks, res_s, rs), (xn, kn, res_n, rn)):
            for which in range(x.shape[0]):
                if step == 0:
                    pieces = [
                        both[pl.ds(own + (first[item] + b) * rank, rank), :]
                        for b in range(widths[item] // LANES)
                    ]
                    mine = jnp.concatenate(pieces, axis=1)
                    (fac_s if x is xs else fac_n)[which] = mine
                    k[which] = wide(mine)
                left = tall(band[item * rank : (item + 1) * rank])
                kept[which, rows] = x[which, rows] - dot(left, k[which], TN)
                out(kept.at[which, rows], r.at[which, rows])
                item += 1

    def velocity():
        item = 0
        for f, m, v, rows_ref in ((fac_s, ms, vel_s, rows_s), (fac_n, mn, vel_n, rows_n)):
            per_row = rows_ref.shape[0]
            rows = m.shape[0] // (f.shape[0] * per_row)
            interleaved = f is fac_n
            at = place * rows
            block, inside = at // LANES, lax.rem(at, LANES)
            for which in range(f.shape[0]):
                full = jnp.concatenate(
                    [factor_of(both, first[item], widths[item], rank, core * blocks) for core in range(2)],
                    axis=1,
                )
                left = tall(ortho[block, item * rank : (item + 1) * rank, :])
                approx = dot(left, wide(full), TN)
                for c in range(per_row):
                    rows_ref[c] = approx[:, c * LANES : (c + 1) * LANES]
                for c in range(per_row):
                    if interleaved:
                        spot = pl.ds(c * f.shape[0] + which, rows, stride=per_row * f.shape[0])
                    else:
                        spot = pl.ds(which * rows * per_row + c, rows, stride=per_row)
                    v[spot, :] = (
                        momentum_decay * m[spot, :]
                        + rows_ref[c, pl.ds(pl.multiple_of(inside, 8), rows), :]
                    )
                item += 1

    steps = xs.shape[1] // BAND
    for step in range(steps):
        residue(step)
        if step == steps - 2:
            velocity()
            for src, dst in ((fac_s, fs), (fac_n, fn), (vel_s, vs), (vel_n, vn)):
                out(src, dst)
    for copy in started:
        copy.wait()


def on_device(gn, en, sn, mn, gs, es, ss, ms):
    replicas = lax.axis_size("rep")
    shape_gn, shape_gs, shape_sn, shape_ss = gn.shape, gs.shape, sn.shape, ss.shape
    shape_mn, shape_ms = mn.shape, ms.shape
    gn, en, gs, es = (
        x.reshape((x.shape[1] * x.shape[2],) + x.shape[3:]) for x in (gn, en, gs, es)
    )
    sn, ss = (jnp.swapaxes(x.reshape((-1,) + x.shape[2:]), 1, 2) for x in (sn, ss))
    cn, depth, wn = gn.shape
    cs, _, ws = gs.shape
    rank = sn.shape[1]
    items = cn + cs
    blocks = depth // LANES
    widths = [ws] * cs + [wn] * cn
    _, all_blocks = first_blocks(widths)
    mn = jnp.swapaxes(mn.reshape(cn, -1, LANES), 0, 1).reshape(-1, LANES)
    ms = ms.reshape(-1, LANES)
    runs = groups_of(widths)

    in_vmem = pl.BlockSpec(memory_space=pltpu.VMEM)
    anywhere = pl.BlockSpec(memory_space=pl.ANY)

    def group_scratch(run):
        size = len(run) * rank
        half_rows, q_rows = blocks // 2 * size, sum(widths[i] for i in run) // LANES * rank
        near = near_size(replicas)
        far = replicas // near
        share, share_q = share_of(half_rows, near), share_of(q_rows, near)
        return [
            pltpu.VMEM((half_rows, LANES), f32),
            pltpu.VMEM((half_rows, LANES), f32),
            pltpu.VMEM((share * near, LANES), f32),
            pltpu.VMEM((2, share * near, LANES), f32),
            pltpu.VMEM((near - 1, share, LANES), f32),
            pltpu.VMEM((far, share, LANES), f32),
            pltpu.VMEM((share_q * near, LANES), f32),
            pltpu.VMEM((share_q * near, LANES), f32),
            pltpu.VMEM((near - 1, share_q, LANES), f32),
            pltpu.VMEM((far, share_q, LANES), f32),
            pltpu.VMEM((size, size), f32),
        ] + [pltpu.SemaphoreType.DMA((2,)) for _ in range(9)]

    scratch = []
    for g, f in ((gs, ss), (gn, sn)):
        twice = (f.shape[0], 2 * rank, f.shape[2])
        scratch += [
            pltpu.VMEM(shape, kind)
            for shape, kind in (
                (g.shape, bf16), (g.shape, f32), (f.shape, f32), (g.shape, bf16), (g.shape, bf16), (twice, bf16)
            )
        ]
    scratch += [pltpu.SemaphoreType.DMA((n,)) for n in (4 * items, 2, 2 * items)]
    for run, _ in runs:
        scratch += group_scratch(run)
    panel_shape = (blocks, items * rank, LANES)
    factor_shape = (2 * all_blocks * rank, LANES)
    xs, xn, ortho, both = pl.pallas_call(
        functools.partial(main_kernel, rank, replicas, runs),
        in_specs=[anywhere] * 6,
        out_specs=[anywhere, anywhere, in_vmem, in_vmem],
        out_shape=[pltpu.VMEM(shape, f32) for shape in (gs.shape, gn.shape, panel_shape, factor_shape)],
        scratch_shapes=scratch,
        compiler_params=pltpu.CompilerParams(
            collective_id=0, has_side_effects=True, vmem_limit_bytes=VMEM_LIMIT
        ),
        name="rounds",
    )(*(pltpu.with_memory_space_constraint(x, pltpu.HBM) for x in (gs, es, ss, gn, en, sn)))

    results = [gs.shape, gn.shape, ss.shape, sn.shape, ms.shape, mn.shape]
    rs, rn, fs, fn, vs, vn = pl.pallas_call(
        functools.partial(last_kernel, rank),
        in_specs=[in_vmem] * 6,
        out_specs=[anywhere] * 6,
        out_shape=[jax.ShapeDtypeStruct(shape, f32) for shape in results],
        scratch_shapes=[
            pltpu.VMEM((cs, 3 * rank, ws), bf16),
            pltpu.VMEM((cn, 3 * rank, wn), bf16),
            pltpu.VMEM((2 * ws // LANES, LANES, LANES), f32),
            pltpu.VMEM((2 * wn // LANES, LANES, LANES), f32),
        ]
        + [pltpu.VMEM(shape, f32) for shape in results]
        + [pltpu.SemaphoreType.DMA((items * (depth // BAND) + 4,))],
        compiler_params=pltpu.CompilerParams(vmem_limit_bytes=LAST_LIMIT),
        name="last",
    )(ortho, both, xs, xn, ms, mn)
    return (
        rn.reshape(shape_gn),
        jnp.swapaxes(fn, 1, 2).reshape(shape_sn),
        jnp.swapaxes(vn.reshape(-1, cn, LANES), 0, 1).reshape(shape_mn),
        rs.reshape(shape_gs),
        jnp.swapaxes(fs, 1, 2).reshape(shape_ss),
        vs.reshape(shape_ms),
    )


def solution(mesh):
    in_specs = (
        P("rep", None, None, None, "tp"),
        P("rep", None, None, None, "tp"),
        P(None, None, "tp", None),
        P(None, None, ("rep", "tp")),
        P("rep", None, None, None, "tp"),
        P("rep", None, None, None, "tp"),
        P(None, None, "tp", None),
        P(None, None, ("rep", "tp")),
    )
    out_specs = (
        P("rep", None, None, None, "tp"),
        P(None, None, "tp", None),
        P(None, None, ("rep", "tp")),
        P("rep", None, None, None, "tp"),
        P(None, None, "tp", None),
        P(None, None, ("rep", "tp")),
    )
    return jax.shard_map(
        on_device, mesh=mesh, in_specs=in_specs, out_specs=out_specs, check_vma=False
    )
```

```python
import functools

import jax
import jax.numpy as jnp
from jax import lax
from jax.experimental import pallas as pl
from jax.experimental.pallas import tpu as pltpu
from jax.sharding import PartitionSpec as P

ROUNDS = 2
NS_STEPS = 5
LANES = 128
BAND = 256
NEAR = 8
AHEAD = 3
VMEM_LIMIT = 40 * 1024 * 1024
LAST_LIMIT = 24 * 1024 * 1024

epsilon = 1e-06
momentum_decay = 0.9
f32, bf16 = jnp.float32, jnp.bfloat16
MESH = pl.DeviceIdType.MESH


def split(x):
    hi = x.astype(bf16)
    lo = (x - hi.astype(f32)).astype(bf16)
    return hi, lo


def dot(a, b, dims):
    return lax.dot_general(a, b, (dims, ((), ())), preferred_element_type=f32)


NN, NT, TN = ((1,), (0,)), ((1,), (1,)), ((0,), (0,))


def dot3(a, b, dims=NN):
    (ah, al), (bh, bl) = split(a), split(b)
    return dot(ah, bh, dims) + (dot(ah, bl, dims) + dot(al, bh, dims))


def rows_at(at, size, unit=8):
    return pl.ds(pl.multiple_of(at, unit), size)


def first_blocks(widths):
    first, at = [], 0
    for width in widths:
        first.append(at)
        at += width // LANES
    return first, at


def factor_of(ref, first, width, rank, offset=0):
    pieces = [
        ref[(offset + first + b) * rank : (offset + first + b + 1) * rank, :]
        for b in range(width // LANES)
    ]
    return jnp.concatenate(pieces, axis=1)


def items_of(square, narrow):
    return [(0, which) for which in range(square)] + [(1, which) for which in range(narrow)]


SPLITS = 3


def groups_of(widths):
    half, total, cut = sum(widths) / 2, 0, len(widths)
    for at, width in enumerate(widths):
        if total >= half:
            cut = at
            break
        total += width
    runs = []
    for team, (start, stop) in enumerate(((0, cut), (cut, len(widths)))):
        count = min(SPLITS, stop - start)
        for part in range(count):
            first = start + part * (stop - start) // count
            last = start + (part + 1) * (stop - start) // count
            runs.append((range(first, last), team))
    return runs


def share_of(rows, parts):
    return -(-rows // (8 * parts)) * 8


def near_size(replicas):
    return NEAR if replicas % NEAR == 0 else replicas


class Group:
    names = (
        "send", "inbox", "mine", "panel", "land", "cross", "part", "total", "landq", "crossq", "turn",
        "side_left", "side_panel", "side_factor", "step_scatter", "step_trade", "step_gather",
        "step_scatter_q", "step_trade_q", "step_gather_q",
    )

    def __init__(self, items, team, refs):
        self.items, self.team = items, team
        for name, ref in zip(self.names, refs):
            setattr(self, name, ref)


def main_kernel(rank, replicas, runs, *refs):
    gs, es, ss, gn, en, sn, out_s, out_n, ortho, both = refs[:10]
    stage_gs, stage_es, stage_ss, hs, ls, fs, stage_gn, stage_en, stage_sn, hn, ln, fn = refs[10:22]
    load_sem, start_sem, save_sem = refs[22:25]
    per = len(Group.names)
    groups = [
        Group(run, team, refs[25 + per * k : 25 + per * (k + 1)]) for k, (run, team) in enumerate(runs)
    ]
    rep, tp = lax.axis_index("rep"), lax.axis_index("tp")
    other = {"rep": rep, "tp": 1 - tp}
    part = hs.shape[1] // 2
    blocks = part // LANES
    kinds = (
        (gs, es, stage_ss, hs, ls, stage_gs, stage_es, fs),
        (gn, en, stage_sn, hn, ln, stage_gn, stage_en, fn),
    )
    items = items_of(hs.shape[0], hn.shape[0])
    widths = [kinds[kind][3].shape[2] for kind, _ in items]
    first_block, all_blocks = first_blocks(widths)

    near = near_size(replicas)
    far = replicas // near
    near_at, far_at = lax.rem(rep, near), rep // near
    near_order = sorted(range(1, near), key=lambda j: -bin(j).count("1"))

    def near_of(j):
        result, bit = 0, 1
        while bit < near:
            here = lax.rem(near_at // bit, 2)
            result = result + bit * (1 - here if j & bit else here)
            bit *= 2
        return result

    def near_peer(j):
        return {"rep": far_at * near + near_of(j), "tp": tp}

    def far_peer(j):
        return {"rep": lax.rem(far_at + j, far) * near + near_at, "tp": tp}

    barrier = pltpu.get_barrier_semaphore()

    partners = [near_peer(j) for j in near_order] + [far_peer(j) for j in range(1, far)] + [other]
    for partner in partners:
        pl.semaphore_signal(barrier, inc=1, device_id=partner, device_id_type=MESH)

    starts = [
        pltpu.make_async_copy(src, dst, start_sem.at[i])
        for i, (src, dst) in enumerate(((ss, stage_ss), (sn, stage_sn)))
    ]
    for copy in starts:
        copy.start()
    def wait_all(copies):
        for copy in copies:
            copy.wait()

    loads, saves = [], []
    for where, half in enumerate((1 - tp, tp)):
        rows = rows_at(half * part, part, LANES)
        for group in groups:
            for item in group.items:
                kind, which = items[item]
                g, e, _, _, _, sg, se, _ = kinds[kind]
                pair = []
                for src, dst in ((g, sg), (e, se)):
                    at = 2 * len(loads) + len(pair)
                    pair.append(
                        pltpu.make_async_copy(src.at[which, rows], dst.at[which, rows], load_sem.at[at])
                    )
                loads.append(pair)
    for pair in loads[:AHEAD]:
        for copy in pair:
            copy.start()
    used = [0]

    def next_load():
        at = used[0]
        used[0] += 1
        for copy in loads[at + AHEAD : at + AHEAD + 1]:
            for one in copy:
                one.start()
        wait_all(loads[at])

    for copy in starts:
        copy.wait()
    for kind, which in items:
        start, keep = kinds[kind][2], kinds[kind][7]
        keep[which] = jnp.concatenate(split(start[which]), axis=0)

    class Flight:
        def __init__(self, slot, all_bytes):
            self.slot, self.all_bytes, self.sent = slot, all_bytes, True

        def wait(self, side):
            pltpu.make_async_copy(self.all_bytes, self.all_bytes, self.slot.at[side]).wait()

    def spread(order, source, target, slot, all_bytes, to):
        for j in order:
            pltpu.make_async_remote_copy(
                src_ref=source(j), dst_ref=target(j), send_sem=slot.at[0], recv_sem=slot.at[1],
                device_id=to(j), device_id_type=MESH,
            ).start()
        return Flight(slot, all_bytes)

    unsent = {}

    def depart(name, flight):
        unsent[name] = flight
        return flight

    def reuse(*names):
        for name in names:
            if name in unsent:
                unsent.pop(name).wait(0)

    def scatter(group, mine, land, slot):
        share = land.shape[1]
        return spread(
            near_order, lambda j: mine.at[rows_at(near_of(j) * share, share)], lambda j: land.at[j - 1],
            slot, land, near_peer,
        )

    def trade(mine, land, cross, slot):
        share = land.shape[1]
        own = rows_at(near_at * share, share)
        value = mine[own, :]
        for j in range(near - 1):
            value = value + land[j]
        cross[far_at] = value
        view = cross.at[far_at]
        return spread(range(1, far), lambda j: view, lambda j: view, slot, cross.at[0 : far - 1], far_peer)

    def gather(cross, whole, slot):
        share = cross.shape[1]
        own = rows_at(near_at * share, share)
        value = cross[0]
        for j in range(1, far):
            value = value + cross[j]
        whole[own, :] = value
        view = whole.at[own]
        return spread(
            near_order, lambda j: view, lambda j: view, slot, whole.at[0 : (near - 1) * share], near_peer
        )

    def to_sibling(src, dst, slot):
        return spread((0,), lambda j: src, lambda j: dst, slot, src, lambda j: other)

    def left_half(group, half, out, fresh):
        size = len(group.items) * rank
        for place, item in enumerate(group.items):
            kind, which = items[item]
            _, _, _, h, l, sg, se, keep = kinds[kind]
            if fresh:
                next_load()
            stacked = keep[which]
            for band in range(part // BAND):
                rows = rows_at(half * part + band * BAND, BAND, LANES)
                if fresh:
                    merged = sg[which, rows, :].astype(f32) + se[which, rows, :]
                    hi, lo = split(merged)
                    se[which, rows, :], h[which, rows, :], l[which, rows, :] = merged, hi, lo
                else:
                    hi, lo = h[which, rows, :], l[which, rows, :]
                twice = dot(stacked, hi, NT)
                result = twice[:rank] + twice[rank:] + dot(stacked[:rank], lo, NT)
                for b in range(BAND // LANES):
                    at = (band * (BAND // LANES) + b) * size + place * rank
                    out[at : at + rank, :] = result[:, b * LANES : (b + 1) * LANES]
            if fresh:
                rows = rows_at(half * part, part, LANES)
                target = (out_s, out_n)[kind]
                copy = pltpu.make_async_copy(se.at[which, rows], target.at[which, rows], save_sem.at[len(saves)])
                copy.start()
                saves.append(copy)

    def panel_half(group, half):
        size = len(group.items) * rank
        return [group.panel[half, b * size : (b + 1) * size, :] for b in range(blocks)]

    def right_half(group, half, first):
        wide = jnp.concatenate(panel_half(group, half), axis=1)
        rows = rows_at(half * part, part, LANES)
        at = 0
        for place, item in enumerate(group.items):
            kind, which = items[item]
            h, l = kinds[kind][3:5]
            hi, lo = split(wide[place * rank : (place + 1) * rank])
            twice = dot(jnp.concatenate([hi, lo], axis=0), h[which, rows, :], NN)
            term = twice[:rank] + twice[rank:] + dot(hi, l[which, rows, :], NN)
            for b in range(widths[item] // LANES):
                piece = term[:, b * LANES : (b + 1) * LANES]
                if first:
                    group.part[at : at + rank, :] = piece
                else:
                    group.part[at : at + rank, :] += piece
                at += rank

    def orthonormal(team, final):
        sizes = [len(group.items) * rank for group in team]
        size = sum(sizes)
        stacked = jnp.concatenate(
            [jnp.concatenate(panel_half(group, 0) + panel_half(group, 1), axis=1) for group in team], axis=0
        )
        row = lax.broadcasted_iota(jnp.int32, (size, size), 0)
        column = lax.broadcasted_iota(jnp.int32, (size, size), 1)
        own = (row // rank) == (column // rank)
        identity = jnp.where(row == column, 1.0, 0.0).astype(f32)
        scale, scaled = [], []
        for place in range(size // rank):
            piece = stacked[place * rank : (place + 1) * rank]
            by = 1.0 / (jnp.sqrt(jnp.sum(piece * piece)) + epsilon)
            scale.append(jnp.full((rank, size), by, f32))
            scaled.append(piece * by)
        scaled = jnp.concatenate(scaled, axis=0)
        gram = jnp.where(own, dot3(scaled, scaled, NT), 0.0)
        total = None
        for sweep in range(NS_STEPS):
            turn = 1.5 * identity - 0.5 * gram
            total = turn if total is None else dot3(turn, total)
            if sweep < NS_STEPS - 1:
                gram = dot3(dot3(turn, gram), turn)
        result = dot3(total, scaled) if final else None
        total = total * jnp.concatenate(scale, axis=0)
        at = 0
        for group, width in zip(team, sizes):
            group.turn[...] = total[at : at + width, at : at + width]
            if final:
                base = group.items[0] * rank
                for b in range(2 * blocks):
                    ortho[b, base : base + width, :] = result[at : at + width, b * LANES : (b + 1) * LANES]
            at += width

    def factors(group):
        at, result = 0, []
        for place, item in enumerate(group.items):
            own = slice(place * rank, (place + 1) * rank)
            pieces = []
            for b in range(widths[item] // LANES):
                pieces.append(group.total[at : at + rank, :])
                at += rank
            turned = dot3(group.turn[own, own] / replicas, jnp.concatenate(pieces, axis=1))
            result.append(turned)
        return result

    flight = [None] * len(groups)
    teams = [[k for k, group in enumerate(groups) if group.team == team] for team in range(2)]
    for turn in range(ROUNDS):
        final = turn == ROUNDS - 1
        across = []
        for k, group in enumerate(groups):
            if turn:
                flight[k].wait(1)
                for item, whole in zip(group.items, factors(group)):
                    kind, which = items[item]
                    kinds[kind][7][which] = jnp.concatenate(split(whole), axis=0)
            reuse((k, "left"), (k, "side"))
            left_half(group, 1 - tp, group.send, not turn)
            if not turn and k == 0:
                pl.semaphore_wait(barrier, len(partners))
            across.append(depart((k, "left"), to_sibling(group.send, group.inbox, group.side_left)))
        for k, group in enumerate(groups):
            reuse((k, "scatter"))
            left_half(group, tp, group.mine, not turn)
            across[k].wait(1)
            used_rows = group.inbox.shape[0]
            group.mine[0:used_rows, :] += group.inbox[...]
            flight[k] = depart((k, "scatter"), scatter(group, group.mine, group.land, group.step_scatter))
        for k, group in enumerate(groups):
            flight[k].wait(1)
            reuse((k, "trade"))
            flight[k] = depart((k, "trade"), trade(group.mine, group.land, group.cross, group.step_trade))
        for k, group in enumerate(groups):
            flight[k].wait(1)
            reuse((k, "gather"))
            flight[k] = depart((k, "gather"), gather(group.cross, group.panel.at[tp], group.step_gather))
        across = []
        for k, group in enumerate(groups):
            flight[k].wait(1)
            view = group.panel.at[tp]
            across.append(depart((k, "side"), to_sibling(view, view, group.side_panel)))
            reuse((k, "scatter_q"))
            right_half(group, tp, True)
        for k, group in enumerate(groups):
            across[k].wait(1)
            right_half(group, 1 - tp, False)
            flight[k] = depart((k, "scatter_q"), scatter(group, group.part, group.landq, group.step_scatter_q))
        orthonormal([groups[k] for k in teams[0]], final)
        for k, group in enumerate(groups):
            flight[k].wait(1)
            reuse((k, "trade_q"))
            flight[k] = depart((k, "trade_q"), trade(group.part, group.landq, group.crossq, group.step_trade_q))
        for k, group in enumerate(groups):
            flight[k].wait(1)
            reuse((k, "gather_q"))
            flight[k] = depart((k, "gather_q"), gather(group.crossq, group.total, group.step_gather_q))
        if teams[1]:
            orthonormal([groups[k] for k in teams[1]], final)
    for k, group in enumerate(groups):
        flight[k].wait(1)
        base = (tp * all_blocks + first_block[group.items[0]]) * rank
        at = 0
        for item, whole in zip(group.items, factors(group)):
            for b in range(widths[item] // LANES):
                both[rows_at(base + at, rank), :] = whole[:, b * LANES : (b + 1) * LANES]
                at += rank
        view = both.at[rows_at(base, at)]
        flight[k] = depart((k, "factor"), to_sibling(view, view, group.side_factor))
    for last in flight:
        last.wait(1)
    reuse(*list(unsent))
    wait_all(saves)


def last_kernel(
    rank, ortho, both, xs, xn, ms, mn, rs, rn, fs, fn, vs, vn,
    ks, kn, rows_s, rows_n, res_s, res_n, fac_s, fac_n, vel_s, vel_n, sem,
):
    widths = [xs.shape[2]] * xs.shape[0] + [xn.shape[2]] * xn.shape[0]
    first, blocks = first_blocks(widths)
    tp = lax.axis_index("tp")
    place = lax.axis_index("rep") * lax.axis_size("tp") + tp
    own = pl.multiple_of(tp * blocks * rank, blocks * rank)
    started = []

    def out(src, dst):
        copy = pltpu.make_async_copy(src, dst, sem.at[len(started)])
        copy.start()
        started.append(copy)

    def wide(whole):
        hi, lo = split(whole)
        return jnp.concatenate([hi, hi, lo], axis=0)

    def tall(part):
        hi, lo = split(part)
        return jnp.concatenate([hi, lo, hi], axis=0)

    def residue(step):
        per = BAND // LANES
        rows = slice(step * BAND, (step + 1) * BAND)
        band = jnp.concatenate([ortho[step * per + b] for b in range(per)], axis=1)
        item = 0
        for x, k, kept, r in ((xs, ks, res_s, rs), (xn, kn, res_n, rn)):
            for which in range(x.shape[0]):
                if step == 0:
                    pieces = [
                        both[pl.ds(own + (first[item] + b) * rank, rank), :]
                        for b in range(widths[item] // LANES)
                    ]
                    mine = jnp.concatenate(pieces, axis=1)
                    (fac_s if x is xs else fac_n)[which] = mine
                    k[which] = wide(mine)
                left = tall(band[item * rank : (item + 1) * rank])
                kept[which, rows] = x[which, rows] - dot(left, k[which], TN)
                out(kept.at[which, rows], r.at[which, rows])
                item += 1

    def velocity():
        item = 0
        for f, m, v, rows_ref in ((fac_s, ms, vel_s, rows_s), (fac_n, mn, vel_n, rows_n)):
            per_row = rows_ref.shape[0]
            rows = m.shape[0] // (f.shape[0] * per_row)
            interleaved = f is fac_n
            at = place * rows
            block, inside = at // LANES, lax.rem(at, LANES)
            for which in range(f.shape[0]):
                full = jnp.concatenate(
                    [factor_of(both, first[item], widths[item], rank, core * blocks) for core in range(2)],
                    axis=1,
                )
                left = tall(ortho[block, item * rank : (item + 1) * rank, :])
                approx = dot(left, wide(full), TN)
                for c in range(per_row):
                    rows_ref[c] = approx[:, c * LANES : (c + 1) * LANES]
                for c in range(per_row):
                    if interleaved:
                        spot = pl.ds(c * f.shape[0] + which, rows, stride=per_row * f.shape[0])
                    else:
                        spot = pl.ds(which * rows * per_row + c, rows, stride=per_row)
                    v[spot, :] = (
                        momentum_decay * m[spot, :]
                        + rows_ref[c, pl.ds(pl.multiple_of(inside, 8), rows), :]
                    )
                item += 1

    steps = xs.shape[1] // BAND
    for step in range(steps):
        residue(step)
        if step == steps - 2:
            velocity()
            for src, dst in ((fac_s, fs), (fac_n, fn), (vel_s, vs), (vel_n, vn)):
                out(src, dst)
    for copy in started:
        copy.wait()


def on_device(gn, en, sn, mn, gs, es, ss, ms):
    replicas = lax.axis_size("rep")
    shape_gn, shape_gs, shape_sn, shape_ss = gn.shape, gs.shape, sn.shape, ss.shape
    shape_mn, shape_ms = mn.shape, ms.shape
    gn, en, gs, es = (
        x.reshape((x.shape[1] * x.shape[2],) + x.shape[3:]) for x in (gn, en, gs, es)
    )
    sn, ss = (jnp.swapaxes(x.reshape((-1,) + x.shape[2:]), 1, 2) for x in (sn, ss))
    cn, depth, wn = gn.shape
    cs, _, ws = gs.shape
    rank = sn.shape[1]
    items = cn + cs
    blocks = depth // LANES
    widths = [ws] * cs + [wn] * cn
    _, all_blocks = first_blocks(widths)
    mn = jnp.swapaxes(mn.reshape(cn, -1, LANES), 0, 1).reshape(-1, LANES)
    ms = ms.reshape(-1, LANES)
    runs = groups_of(widths)

    in_vmem = pl.BlockSpec(memory_space=pltpu.VMEM)
    anywhere = pl.BlockSpec(memory_space=pl.ANY)

    def group_scratch(run):
        size = len(run) * rank
        half_rows, q_rows = blocks // 2 * size, sum(widths[i] for i in run) // LANES * rank
        near = near_size(replicas)
        far = replicas // near
        share, share_q = share_of(half_rows, near), share_of(q_rows, near)
        return [
            pltpu.VMEM((half_rows, LANES), f32),
            pltpu.VMEM((half_rows, LANES), f32),
            pltpu.VMEM((share * near, LANES), f32),
            pltpu.VMEM((2, share * near, LANES), f32),
            pltpu.VMEM((near - 1, share, LANES), f32),
            pltpu.VMEM((far, share, LANES), f32),
            pltpu.VMEM((share_q * near, LANES), f32),
            pltpu.VMEM((share_q * near, LANES), f32),
            pltpu.VMEM((near - 1, share_q, LANES), f32),
            pltpu.VMEM((far, share_q, LANES), f32),
            pltpu.VMEM((size, size), f32),
        ] + [pltpu.SemaphoreType.DMA((2,)) for _ in range(9)]

    scratch = []
    for g, f in ((gs, ss), (gn, sn)):
        twice = (f.shape[0], 2 * rank, f.shape[2])
        scratch += [
            pltpu.VMEM(shape, kind)
            for shape, kind in (
                (g.shape, bf16), (g.shape, f32), (f.shape, f32), (g.shape, bf16), (g.shape, bf16), (twice, bf16)
            )
        ]
    scratch += [pltpu.SemaphoreType.DMA((n,)) for n in (4 * items, 2, 2 * items)]
    for run, _ in runs:
        scratch += group_scratch(run)
    panel_shape = (blocks, items * rank, LANES)
    factor_shape = (2 * all_blocks * rank, LANES)
    xs, xn, ortho, both = pl.pallas_call(
        functools.partial(main_kernel, rank, replicas, runs),
        in_specs=[anywhere] * 6,
        out_specs=[anywhere, anywhere, in_vmem, in_vmem],
        out_shape=[pltpu.VMEM(shape, f32) for shape in (gs.shape, gn.shape, panel_shape, factor_shape)],
        scratch_shapes=scratch,
        compiler_params=pltpu.CompilerParams(
            collective_id=0, has_side_effects=True, vmem_limit_bytes=VMEM_LIMIT
        ),
        name="rounds",
    )(*(pltpu.with_memory_space_constraint(x, pltpu.HBM) for x in (gs, es, ss, gn, en, sn)))

    results = [gs.shape, gn.shape, ss.shape, sn.shape, ms.shape, mn.shape]
    rs, rn, fs, fn, vs, vn = pl.pallas_call(
        functools.partial(last_kernel, rank),
        in_specs=[in_vmem] * 6,
        out_specs=[anywhere] * 6,
        out_shape=[jax.ShapeDtypeStruct(shape, f32) for shape in results],
        scratch_shapes=[
            pltpu.VMEM((cs, 3 * rank, ws), bf16),
            pltpu.VMEM((cn, 3 * rank, wn), bf16),
            pltpu.VMEM((2 * ws // LANES, LANES, LANES), f32),
            pltpu.VMEM((2 * wn // LANES, LANES, LANES), f32),
        ]
        + [pltpu.VMEM(shape, f32) for shape in results]
        + [pltpu.SemaphoreType.DMA((items * (depth // BAND) + 4,))],
        compiler_params=pltpu.CompilerParams(vmem_limit_bytes=LAST_LIMIT),
        name="last",
    )(ortho, both, xs, xn, ms, mn)
    return (
        rn.reshape(shape_gn),
        jnp.swapaxes(fn, 1, 2).reshape(shape_sn),
        jnp.swapaxes(vn.reshape(-1, cn, LANES), 0, 1).reshape(shape_mn),
        rs.reshape(shape_gs),
        jnp.swapaxes(fs, 1, 2).reshape(shape_ss),
        vs.reshape(shape_ms),
    )


def solution(mesh):
    in_specs = (
        P("rep", None, None, None, "tp"),
        P("rep", None, None, None, "tp"),
        P(None, None, "tp", None),
        P(None, None, ("rep", "tp")),
        P("rep", None, None, None, "tp"),
        P("rep", None, None, None, "tp"),
        P(None, None, "tp", None),
        P(None, None, ("rep", "tp")),
    )
    out_specs = (
        P("rep", None, None, None, "tp"),
        P(None, None, "tp", None),
        P(None, None, ("rep", "tp")),
        P("rep", None, None, None, "tp"),
        P(None, None, "tp", None),
        P(None, None, ("rep", "tp")),
    )
    return jax.shard_map(
        on_device, mesh=mesh, in_specs=in_specs, out_specs=out_specs, check_vma=False
    )
```
